32 devices in a mesh: shard: 4 (over y, x), replica: 8 (over z, core).
Axes of the slice: x: 2, y: 2, z: 4, core: 2. Of those that a mesh axis runs over, the one named last changes fastest.
Arguments:
- images: float32 [32, 197, 384], P(('shard', 'replica')), may hold values from -6 to 6
- cotangent: float32 [32, 197, 384], P(('shard', 'replica')), may hold values from -6 to 6
- counts: int32 [32], P(('shard', 'replica')), may hold values from 0 to 1, as said below
- w_qkv: bfloat16 [2, 384, 1152], P(None, 'shard'), may hold values from -0.3125 to 0.3125
- w_out: bfloat16 [2, 384, 384], P(None, 'shard'), may hold values from -1.25 to 1.25
- w_up: bfloat16 [2, 384, 1536], P(None, 'shard'), may hold values from -0.3125 to 0.3125
- w_down: bfloat16 [2, 1536, 384], P(None, 'shard'), may hold values from -0.15625 to 0.15625
- gains: bfloat16 [2, 2, 384], P(None, None, 'shard'), may hold values from 0.25 to 1.75
- biases: bfloat16 [2, 6, 384], P(None, None, 'shard'), may hold values from -1.796875 to 1.796875
- up_bias: bfloat16 [2, 1536], P(None, 'shard'), may hold values from -1.796875 to 1.796875
Outputs:
- activations: float32 [32, 197, 384], P(('shard', 'replica'))
- input_grad: float32 [32, 197, 384], P(('shard', 'replica'))
- grad_qkv: float32 [2, 384, 1152], P(None, 'shard')
- grad_out: float32 [2, 384, 384], P(None, 'shard')
- grad_up: float32 [2, 384, 1536], P(None, 'shard')
- grad_down: float32 [2, 1536, 384], P(None, 'shard')
- grad_gains: float32 [2, 2, 384], P(None, None, 'shard')
- grad_biases: float32 [2, 6, 384], P(None, None, 'shard')
- grad_upbias: float32 [2, 1536], P(None, 'shard')
The draws below stay inside these ranges and needn't reach their ends.
Inputs may be any that keep to these rules, and one draw needn't show every extreme that they name: `counts`: some device has all 1 slots live and some other device has none.
All inputs are finite; a program needn't handle non-finite values.
Results may differ from the reference program's by a relative error of at most 0.018.
Values may be sent and summed in bfloat16 or wider, within the bound.
A program may use at most 128 MiB of HBM per device.

```python
import jax
import jax.numpy as jnp
from jax import lax

D = 384
HEADS = 6
FF = 1536
HD = 64
S = 197
LAYERS = 2
IMG_DEV = 1
HOLDERS = 32
SLOTS = 32


def draw_counts(key, part):
    first, second, third = jax.random.split(jax.random.fold_in(key, 7), 3)
    filled = jax.random.randint(first, (HOLDERS,), 0, IMG_DEV + 1)
    where = jax.random.randint(second, (), 0, HOLDERS)
    offset = jax.random.randint(third, (), 1, HOLDERS)
    other = (where + offset) % HOLDERS
    filled = filled.at[where].set(IMG_DEV)
    filled = filled.at[other].set(0)
    return filled.astype(jnp.int32)


def levels(stream_key, extent, shards, smallest, high):
    def one(position, shards_of):
        steps = jax.random.uniform(jax.random.fold_in(jax.random.fold_in(stream_key, 6), position), (shards_of,), jnp.float32, smallest / len(shards), high / len(shards))
        return jnp.repeat(jnp.exp(steps), extent[position] // shards_of).reshape((-1,) + (1,) * (len(extent) - position - 1))

    level = one(*shards[0])
    for cut in shards[1:]:
        level = level * one(*cut)
    return level


def bell_draw(rng, shape, deviation, bound, cuts=(), held_as=jnp.bfloat16):
    loudness = levels(rng, shape, cuts, -0.22, 0.18) if cuts else 1.0
    values = jax.random.normal(rng, shape, jnp.float32) * deviation * loudness
    return jnp.minimum(jnp.maximum(values, -bound), bound).astype(held_as)


def setup_inputs(seed: int = 0) -> dict:
    keys = jax.random.split(jax.random.key(seed), 11)
    return {
        "images": bell_draw(keys[0], (SLOTS, S, D), 1.0, 6.0, ((0, 32),), jnp.float32),
        "cotangent": bell_draw(keys[1], (SLOTS, S, D), 1.0, 6.0, ((0, 32),), jnp.float32),
        "counts": draw_counts(jax.random.fold_in(keys[10], 71), 0),
        "w_qkv": bell_draw(keys[3], (LAYERS, D, 3 * D), D ** -0.5, 0.3125, ((1, 4),)),
        "w_out": bell_draw(keys[4], (LAYERS, D, D), (D // 16) ** -0.5, 1.25, ((1, 4),)),
        "w_up": bell_draw(keys[5], (LAYERS, D, FF), D ** -0.5, 0.3125, ((1, 4),)),
        "w_down": bell_draw(keys[6], (LAYERS, FF, D), FF ** -0.5, 0.15625, ((1, 4),)),
        "gains": jnp.clip(1.0 + 0.15 * jax.random.normal(keys[7], (LAYERS, 2, D), jnp.float32), 0.25, 1.75).astype(jnp.bfloat16),
        "biases": bell_draw(keys[8], (LAYERS, 6, D), 0.3, 1.796875, ((2, 4),)),
        "up_bias": bell_draw(keys[9], (LAYERS, FF), 0.3, 1.796875, ((1, 4),)),
    }


EPS = 1e-06
INV_ROOT_TWO = 0.7071067811865476
INV_ROOT_TWO_PI = 0.3989422804014327

def normalize(values, gain, shift):
    center = lax.optimization_barrier(jnp.mean(values, -1, keepdims=True))
    centered = values - center
    spread = lax.optimization_barrier(jnp.mean(centered * centered, -1, keepdims=True))
    inverse = lax.rsqrt(spread + EPS)
    unit = centered * inverse
    return (unit * gain + shift, unit, inverse)

def norm_back(upstream, unit, inverse, gain):
    scaled = upstream * gain
    inner = scaled - lax.optimization_barrier(jnp.mean(scaled, -1, keepdims=True)) - unit * lax.optimization_barrier(jnp.mean(scaled * unit, -1, keepdims=True))
    return (inverse * inner, lax.optimization_barrier(jnp.sum(upstream * unit, 0)), lax.optimization_barrier(jnp.sum(upstream, 0)))

def normal_cdf(values):
    return 0.5 * (1.0 + jax.scipy.special.erf(values * INV_ROOT_TWO))

def product(left, right):
    return jnp.dot(left, right, preferred_element_type=jnp.float32)

def product_left(left, right):
    return jnp.dot(left.T, right, preferred_element_type=jnp.float32)

def product_right(left, right):
    return jnp.dot(left, right.T, preferred_element_type=jnp.float32)

def batched(form, left, right):
    return jnp.einsum(form, left.astype(jnp.float32), right.astype(jnp.float32))

def inner_layer(stream, params, log_total):
    w_qkv, w_out, w_up, w_down, gains, biases, up_bias = params
    gains = gains.astype(jnp.float32)
    biases = biases.astype(jnp.float32)
    up_bias = up_bias.astype(jnp.float32)
    blocks = stream.shape[0]
    factor = HD ** (-0.5)
    rows_in = stream.reshape(-1, D)
    normed_f, unit_one, scale_one = normalize(rows_in, gains[0], biases[0])
    normed_one = normed_f.astype(jnp.bfloat16)
    project = product(normed_one, w_qkv)
    queries = ((project[:, :D] + biases[1]) * factor).astype(jnp.bfloat16).reshape(blocks, S, HEADS, HD)
    key_rows = project[:, D:2 * D].astype(jnp.bfloat16).reshape(blocks, S, HEADS, HD)
    values = (project[:, 2 * D:] + biases[2]).astype(jnp.bfloat16).reshape(blocks, S, HEADS, HD)
    scores = batched('bqhe,bkhe->bhqk', queries, key_rows)
    if log_total is None:
        log_total = jnp.log(lax.optimization_barrier(jnp.sum(jnp.exp(scores), -1, keepdims=True)))
    probs = jnp.exp(scores - log_total)
    prob_low = probs.astype(jnp.bfloat16)
    mixed = batched('bhqk,bkhe->bqhe', prob_low, values).reshape(-1, D).astype(jnp.bfloat16)
    middle = rows_in + product(mixed, w_out) + biases[3]
    normed_g, unit_two, scale_two = normalize(middle, gains[1], biases[4])
    normed_two = normed_g.astype(jnp.bfloat16)
    hidden = product(normed_two, w_up) + up_bias
    activated = (hidden * normal_cdf(hidden)).astype(jnp.bfloat16)
    result = middle + product(activated, w_down) + biases[5]
    saved = (normed_one, unit_one, scale_one, queries, key_rows, values, probs, prob_low, mixed, normed_two, unit_two, scale_two, hidden, activated)
    return (result.reshape(stream.shape), log_total, saved)

def backward_layer(stream, log_total, grad, params):
    w_qkv, w_out, w_up, w_down, gains, biases, up_bias = params
    gains_f = gains.astype(jnp.float32)
    blocks = stream.shape[0]
    factor = HD ** (-0.5)
    _, _, saved = inner_layer(stream, params, log_total)
    normed_one, unit_one, scale_one, queries, key_rows, values, probs, prob_low, mixed, normed_two, unit_two, scale_two, hidden, activated = saved
    low = grad.astype(jnp.bfloat16)
    down_grad = product_left(activated, low)
    shift_five = lax.optimization_barrier(jnp.sum(grad, 0))
    act_grad = product_right(low, w_down)
    dens = jnp.exp(-0.5 * hidden * hidden) * INV_ROOT_TWO_PI
    hid_grad = act_grad * (normal_cdf(hidden) + hidden * dens)
    hid_low = hid_grad.astype(jnp.bfloat16)
    up_grad = product_left(normed_two, hid_low)
    upbias_grad = lax.optimization_barrier(jnp.sum(hid_grad, 0))
    norm_grad = product_right(hid_low, w_up)
    back_two, gain_two, shift_four = norm_back(norm_grad, unit_two, scale_two, gains_f[1])
    mid_grad = grad + back_two
    mid_low = mid_grad.astype(jnp.bfloat16)
    out_grad = product_left(mixed, mid_low)
    shift_three = lax.optimization_barrier(jnp.sum(mid_grad, 0))
    mixed_grad = product_right(mid_low, w_out).astype(jnp.bfloat16).reshape(blocks, S, HEADS, HD)
    prob_grad = batched('bqhe,bkhe->bhqk', mixed_grad, values)
    row_dot = lax.optimization_barrier(jnp.sum(probs * prob_grad, -1, keepdims=True))
    score_grad = (probs * (prob_grad - row_dot)).astype(jnp.bfloat16)
    query_grad = (batched('bhqk,bkhe->bqhe', score_grad, key_rows) * factor).reshape(-1, D)
    key_grad = batched('bhqk,bqhe->bkhe', score_grad, queries).reshape(-1, D)
    value_grad = batched('bhqk,bqhe->bkhe', prob_low, mixed_grad).reshape(-1, D)
    project_grad = jnp.concatenate([query_grad, key_grad, value_grad], 1).astype(jnp.bfloat16)
    qkv_grad = product_left(normed_one, project_grad)
    first_grad = product_right(project_grad, w_qkv)
    back_one, gain_one, shift_zero = norm_back(first_grad, unit_one, scale_one, gains_f[0])
    stream_grad = mid_grad + back_one
    grads = (qkv_grad, out_grad, up_grad, down_grad, jnp.stack([gain_one, gain_two], 0), jnp.stack([shift_zero, lax.optimization_barrier(jnp.sum(query_grad, 0)), lax.optimization_barrier(jnp.sum(value_grad, 0)), shift_three, shift_four, shift_five], 0), upbias_grad)
    return (stream_grad, grads)

def reference(images, cotangent, counts, w_qkv, w_out, w_up, w_down, gains, biases, up_bias):
    stacks = (w_qkv, w_out, w_up, w_down, gains, biases, up_bias)
    image_blocks = images.reshape(HOLDERS, IMG_DEV, S, D)
    cot_blocks = cotangent.reshape(HOLDERS, IMG_DEV, S, D)
    starting = tuple((jnp.zeros(stack.shape, jnp.float32) for stack in stacks))

    def step(totals, item):
        block, cot_block, count = item
        live = (jnp.arange(IMG_DEV, dtype=jnp.int32) < count).astype(jnp.float32)[:, None, None]
        stream = block
        kept = []
        for layer in range(LAYERS):
            params = tuple((stack[layer] for stack in stacks))
            result, log_total, _ = inner_layer(stream, params, None)
            kept.append((stream, log_total))
            stream = result
        output = stream * live
        grad = (cot_block * live).reshape(-1, D)
        totals = list(totals)
        for layer in reversed(range(LAYERS)):
            params = tuple((stack[layer] for stack in stacks))
            grad, grads = backward_layer(kept[layer][0], kept[layer][1], grad, params)
            totals = [total.at[layer].add(piece) for total, piece in zip(totals, grads)]
        return (tuple(totals), (output, grad.reshape(IMG_DEV, S, D)))
    totals, (outputs, grads_in) = lax.scan(step, starting, (image_blocks, cot_blocks, counts))
    activations = outputs.reshape(SLOTS, S, D)
    input_grad = grads_in.reshape(SLOTS, S, D)
    return (activations, input_grad, totals[0], totals[1], totals[2], totals[3], totals[4], totals[5], totals[6])
```

```python
import functools

import jax
import jax.numpy as jnp
from jax import lax
from jax.experimental import pallas as pl
from jax.experimental.pallas import tpu as pltpu
from jax.sharding import PartitionSpec as P

D = 384
HEADS = 6
HD = 64
S = 197
LAYERS = 2


EPS = 1e-06
INV_ROOT_TWO = 0.7071067811865476
INV_ROOT_TWO_PI = 0.3989422804014327


def normalize(values, gain, shift):
    center = jnp.mean(values, -1, keepdims=True)
    centered = values - center
    spread = jnp.mean(centered * centered, -1, keepdims=True)
    inverse = lax.rsqrt(spread + EPS)
    unit = centered * inverse
    return (unit * gain + shift, unit, inverse)


def norm_back(upstream, unit, inverse, gain):
    scaled = upstream * gain
    inner = (
        scaled
        - jnp.mean(scaled, -1, keepdims=True)
        - unit * jnp.mean(scaled * unit, -1, keepdims=True)
    )
    return (inverse * inner, jnp.sum(upstream * unit, 0), jnp.sum(upstream, 0))


def normal_cdf(values):
    return 0.5 * (1.0 + jax.scipy.special.erf(values * INV_ROOT_TWO))


def product(left, right):
    return jnp.dot(left, right, preferred_element_type=jnp.float32)


def product_left(left, right):
    return lax.dot_general(
        left, right, (((0,), (0,)), ((), ())), preferred_element_type=jnp.float32
    )


def product_right(left, right):
    return lax.dot_general(
        left, right, (((1,), (1,)), ((), ())), preferred_element_type=jnp.float32
    )


def batched(form, left, right):
    return jnp.einsum(form, left, right, preferred_element_type=jnp.float32)


def forward_layer(stream, params):
    w_qkv, w_out, w_up, w_down, gains, biases, up_bias = params
    gains = gains.astype(jnp.float32)
    biases = biases.astype(jnp.float32)
    up_bias = up_bias.astype(jnp.float32)
    blocks = stream.shape[0]
    factor = HD ** (-0.5)
    rows_in = stream.reshape(-1, D)
    normed_f, unit_one, scale_one = normalize(rows_in, gains[0], biases[0])
    normed_one = normed_f.astype(jnp.bfloat16)
    project = product(normed_one, w_qkv)
    queries = (
        ((project[:, :D] + biases[1]) * factor).astype(jnp.bfloat16).reshape(blocks, S, HEADS, HD)
    )
    key_rows = project[:, D : 2 * D].astype(jnp.bfloat16).reshape(blocks, S, HEADS, HD)
    values = (project[:, 2 * D :] + biases[2]).astype(jnp.bfloat16).reshape(blocks, S, HEADS, HD)
    scores = batched("bqhe,bkhe->bhqk", queries, key_rows)
    log_total = jnp.log(jnp.sum(jnp.exp(scores), -1, keepdims=True))
    probs = jnp.exp(scores - log_total)
    prob_low = probs.astype(jnp.bfloat16)
    mixed = batched("bhqk,bkhe->bqhe", prob_low, values).reshape(-1, D).astype(jnp.bfloat16)
    middle = rows_in + product(mixed, w_out) + biases[3]
    normed_g, unit_two, scale_two = normalize(middle, gains[1], biases[4])
    normed_two = normed_g.astype(jnp.bfloat16)
    hidden = product(normed_two, w_up) + up_bias
    activated = (hidden * normal_cdf(hidden)).astype(jnp.bfloat16)
    result = middle + product(activated, w_down) + biases[5]
    saved = (
        normed_one,
        unit_one,
        scale_one,
        queries,
        key_rows,
        values,
        log_total,
        mixed,
        normed_two,
        unit_two,
        scale_two,
        hidden,
        activated,
    )
    return (result.reshape(stream.shape), saved)


def backward_layer(saved, grad, params):
    w_qkv, w_out, w_up, w_down, gains, biases, up_bias = params
    gains_f = gains.astype(jnp.float32)
    factor = HD ** (-0.5)
    (
        normed_one,
        unit_one,
        scale_one,
        queries,
        key_rows,
        values,
        log_total,
        mixed,
        normed_two,
        unit_two,
        scale_two,
        hidden,
        activated,
    ) = saved
    blocks = queries.shape[0]
    low = grad.astype(jnp.bfloat16)
    down_grad = product_left(activated, low)
    shift_five = jnp.sum(grad, 0)
    act_grad = product_right(low, w_down)
    dens = jnp.exp(-0.5 * hidden * hidden) * INV_ROOT_TWO_PI
    hid_grad = act_grad * (normal_cdf(hidden) + hidden * dens)
    hid_low = hid_grad.astype(jnp.bfloat16)
    up_grad = product_left(normed_two, hid_low)
    upbias_grad = jnp.sum(hid_grad, 0)
    norm_grad = product_right(hid_low, w_up)
    back_two, gain_two, shift_four = norm_back(norm_grad, unit_two, scale_two, gains_f[1])
    mid_grad = grad + back_two
    mid_low = mid_grad.astype(jnp.bfloat16)
    out_grad = product_left(mixed, mid_low)
    shift_three = jnp.sum(mid_grad, 0)
    mixed_grad = product_right(mid_low, w_out).astype(jnp.bfloat16).reshape(blocks, S, HEADS, HD)
    scores = batched("bqhe,bkhe->bhqk", queries, key_rows)
    probs = jnp.exp(scores - log_total)
    prob_low = probs.astype(jnp.bfloat16)
    prob_grad = batched("bqhe,bkhe->bhqk", mixed_grad, values)
    row_dot = jnp.sum(probs * prob_grad, -1, keepdims=True)
    score_grad = (probs * (prob_grad - row_dot)).astype(jnp.bfloat16)
    query_grad = (batched("bhqk,bkhe->bqhe", score_grad, key_rows) * factor).reshape(-1, D)
    key_grad = batched("bhqk,bqhe->bkhe", score_grad, queries).reshape(-1, D)
    value_grad = batched("bhqk,bqhe->bkhe", prob_low, mixed_grad).reshape(-1, D)
    project_grad = jnp.concatenate([query_grad, key_grad, value_grad], 1).astype(jnp.bfloat16)
    qkv_grad = product_left(normed_one, project_grad)
    first_grad = product_right(project_grad, w_qkv)
    back_one, gain_one, shift_zero = norm_back(first_grad, unit_one, scale_one, gains_f[0])
    stream_grad = mid_grad + back_one
    grads = (
        qkv_grad,
        out_grad,
        up_grad,
        down_grad,
        jnp.stack([gain_one, gain_two], 0),
        jnp.stack(
            [
                shift_zero,
                jnp.sum(query_grad, 0),
                jnp.sum(value_grad, 0),
                shift_three,
                shift_four,
                shift_five,
            ],
            0,
        ),
        upbias_grad,
    )
    return (stream_grad, grads)


MESH = pl.DeviceIdType.MESH


def place(shards, replicas):
    me = lax.axis_index("shard")
    rep = lax.axis_index("replica")
    core = lax.rem(rep, 2)
    depth = lax.div(rep, 2)
    return me, rep, core, depth, rep + 1 - 2 * core


def gather_kernel(shards, layers, count, *refs):
    ins = refs[: count + 1]
    outs = refs[count + 1 : count + 2 + count * layers]
    send, recv, psend, precv, ssend, srecv, local = refs[count + 2 + count * layers :]
    me, rep, core, depth, mate = place(shards, 0)
    barrier = pltpu.get_barrier_semaphore()
    pl.semaphore_signal(barrier, inc=1, device_id=(me, mate), device_id_type=MESH)
    for k in range(1, shards):
        peer = lax.rem(me + k, shards)
        pl.semaphore_signal(barrier, inc=1, device_id=(peer, rep), device_id_type=MESH)
    pl.semaphore_wait(barrier, shards)
    small_in, small_out = ins[count], outs[count * layers]
    smalls = []
    for k in range(1, shards):
        peer = lax.rem(me + k, shards)
        copy = pltpu.make_async_remote_copy(
            src_ref=small_in, dst_ref=small_out.at[me], send_sem=ssend.at[k - 1],
            recv_sem=srecv.at[k - 1], device_id=(peer, rep), device_id_type=MESH)
        copy.start()
        smalls.append(copy)
    first = []
    for layer in range(layers):
        for a in range(count):
            item = layer * count + a
            for k in range(1, shards):
                peer = lax.rem(me + k, shards)
                copy = pltpu.make_async_remote_copy(
                    src_ref=ins[a].at[layer, core], dst_ref=outs[item].at[me, core],
                    send_sem=send.at[item, k - 1], recv_sem=recv.at[item, k - 1],
                    device_id=(peer, rep), device_id_type=MESH)
                copy.start()
                first.append((item, k, copy))
    own = []
    for layer in range(layers):
        for a in range(count):
            item = layer * count + a
            copy = pltpu.make_async_copy(ins[a].at[layer], outs[item].at[me], local.at[item])
            copy.start()
            own.append(copy)
    copy = pltpu.make_async_copy(small_in, small_out.at[me], local.at[layers * count])
    copy.start()
    own.append(copy)
    second = []
    for item, k, copy in first:
        origin = lax.rem(me + shards - k, shards)
        copy.wait_recv()
        piece = outs[item].at[origin, core]
        passed = pltpu.make_async_remote_copy(
            src_ref=piece, dst_ref=piece, send_sem=psend.at[item, k - 1],
            recv_sem=precv.at[item, k - 1], device_id=(me, mate), device_id_type=MESH)
        passed.start()
        second.append(passed)
    for copy in smalls:
        copy.wait()
    for copy in own:
        copy.wait()
    for item, k, copy in first:
        copy.wait_send()
    for copy in second:
        copy.wait()


def gather(stacks, shards):
    weights = stacks[:4]
    layers = weights[0].shape[0]
    ins = [w.reshape(layers, 2, w.shape[1] // 2, w.shape[2]) for w in weights]
    gains, biases, up_bias = stacks[4:]
    width = gains.shape[2]
    small = jnp.concatenate([gains, biases, up_bias.reshape(layers, -1, width)], 1)
    rows = small.shape[1]
    small = jnp.pad(small, ((0, 0), (0, -rows % 16), (0, -width % 128)))
    count = len(ins)
    shapes = [
        jax.ShapeDtypeStruct((shards,) + w.shape[1:], w.dtype) for _ in range(layers) for w in ins
    ]
    shapes.append(jax.ShapeDtypeStruct((shards,) + small.shape, small.dtype))
    sems = pltpu.SemaphoreType.DMA
    items = layers * count
    outs = pl.pallas_call(
        functools.partial(gather_kernel, shards, layers, count),
        out_shape=shapes,
        in_specs=[pl.BlockSpec(memory_space=pltpu.VMEM)] * (count + 1),
        out_specs=[pl.BlockSpec(memory_space=pl.ANY)] * len(shapes),
        scratch_shapes=[
            sems((items, shards - 1)), sems((items, shards - 1)),
            sems((items, shards - 1)), sems((items, shards - 1)),
            sems((shards - 1,)), sems((shards - 1,)), sems((items + 1,)),
        ],
        compiler_params=pltpu.CompilerParams(collective_id=0, has_side_effects=True),
        name="gather_params",
    )(*ins, small)
    tiny = outs[-1][:, :, :rows, :width]
    params = []
    for layer in range(layers):
        big = [outs[layer * count + a].reshape(-1, weights[a].shape[2]) for a in range(count)]
        part = tiny[:, layer]
        ng, nb = gains.shape[1], biases.shape[1]
        params.append(tuple(big) + (
            part[:, :ng].transpose(1, 0, 2).reshape(ng, -1),
            part[:, ng : ng + nb].transpose(1, 0, 2).reshape(nb, -1),
            part[:, ng + nb :].reshape(-1),
        ))
    return params


def blocks_of(shape):
    return [(r, c) for r in range(shape[0] // BLOCK) for c in range(shape[1] // 128)]


def reduce_kernel(shards, deep, per, count, *refs):
    ins, outs = refs[:count], refs[count : 2 * count]
    refs = refs[2 * count :]
    buf_a, buf_s, buf_b = refs[:count], refs[count : 2 * count], refs[2 * count : 3 * count]
    z_own, z_recv, z_sum, z_all, z_mate = refs[3 * count : 3 * count + 5]
    a_send, a_recv, b_send, b_recv, c_send, c_recv, d_send, d_recv, e_send, e_recv, loc = refs[
        3 * count + 5 :
    ]
    me, rep, core, depth, mate = place(shards, deep)
    barrier = pltpu.get_barrier_semaphore()
    pl.semaphore_signal(barrier, inc=1, device_id=(me, mate), device_id_type=MESH)
    for k in range(1, shards):
        peer = lax.rem(me + k, shards)
        pl.semaphore_signal(barrier, inc=1, device_id=(peer, rep), device_id_type=MESH)
    for k in range(1, deep):
        peer = lax.rem(depth + k, deep) * 2 + core
        pl.semaphore_signal(barrier, inc=1, device_id=(me, peer), device_id_type=MESH)
    pl.semaphore_wait(barrier, shards + deep - 1)

    stage_a = []
    for a in range(count):
        copy = pltpu.make_async_remote_copy(
            src_ref=ins[a].at[:, 1 - core], dst_ref=buf_a[a], send_sem=a_send.at[a],
            recv_sem=a_recv.at[a], device_id=(me, mate), device_id_type=MESH)
        copy.start()
        stage_a.append(copy)
    stage_b = []
    for a in range(count):
        stage_a[a].wait_recv()
        for k in list(range(1, shards)) + [0]:
            peer = lax.rem(me + k, shards)
            mine = ins[a][peer, core].astype(jnp.float32)
            buf_s[a][peer] = (mine + buf_a[a][peer].astype(jnp.float32)).astype(jnp.bfloat16)
            if k:
                copy = pltpu.make_async_remote_copy(
                    src_ref=buf_s[a].at[peer], dst_ref=buf_b[a].at[k - 1],
                    send_sem=b_send.at[a, k - 1], recv_sem=b_recv.at[a, k - 1],
                    device_id=(peer, rep), device_id_type=MESH)
                copy.start()
                stage_b.append((a, copy))
    number = 0
    for a in range(count):
        for owner, copy in stage_b:
            if owner == a:
                copy.wait_recv()
        for r, c in blocks_of(buf_s[a].shape[1:]):
            rows, cols = pl.ds(r * BLOCK, BLOCK), pl.ds(c * 128, 128)
            total = buf_s[a][me, rows, cols].astype(jnp.float32)
            for k in range(shards - 1):
                total = total + buf_b[a][k, rows, cols].astype(jnp.float32)
            z_own[number // per, number % per] = total.astype(jnp.bfloat16)
            number += 1
    while number < deep * per:
        z_own[number // per, number % per] = jnp.zeros((BLOCK, 128), jnp.bfloat16)
        number += 1
    stage_c = []
    for k in range(1, deep):
        peer = lax.rem(depth + k, deep)
        copy = pltpu.make_async_remote_copy(
            src_ref=z_own.at[peer], dst_ref=z_recv.at[k - 1], send_sem=c_send.at[k - 1],
            recv_sem=c_recv.at[k - 1], device_id=(me, peer * 2 + core), device_id_type=MESH)
        copy.start()
        stage_c.append(copy)
    for copy in stage_c:
        copy.wait_recv()
    for b in range(per):
        total = z_own[depth, b].astype(jnp.float32)
        for k in range(deep - 1):
            total = total + z_recv[k, b].astype(jnp.float32)
        z_sum[b] = total.astype(jnp.bfloat16)
    stage_d = []
    for k in range(1, deep):
        peer = lax.rem(depth + k, deep)
        copy = pltpu.make_async_remote_copy(
            src_ref=z_sum, dst_ref=z_all.at[depth], send_sem=d_send.at[k - 1],
            recv_sem=d_recv.at[k - 1], device_id=(me, peer * 2 + core), device_id_type=MESH)
        copy.start()
        stage_d.append(copy)
    own = pltpu.make_async_copy(z_sum, z_all.at[depth], loc.at[0])
    own.start()
    own.wait()
    stage_e = []
    for k in range(deep):
        origin = lax.rem(depth + deep - k, deep)
        if k:
            stage_d[k - 1].wait_recv()
        copy = pltpu.make_async_remote_copy(
            src_ref=z_all.at[origin], dst_ref=z_mate.at[origin], send_sem=e_send.at[k],
            recv_sem=e_recv.at[k], device_id=(me, mate), device_id_type=MESH)
        copy.start()
        stage_e.append(copy)

    def put(held, half):
        at = 0
        for a in range(count):
            for r, c in blocks_of(outs[a].shape[1:]):
                rows, cols = pl.ds(r * BLOCK, BLOCK), pl.ds(c * 128, 128)
                outs[a][half, rows, cols] = held[at // per, at % per].astype(jnp.float32)
                at += 1

    put(z_all, core)
    for copy in stage_e:
        copy.wait_recv()
    put(z_mate, 1 - core)
    for copy in stage_a + [c for _, c in stage_b] + stage_c + stage_d + stage_e:
        copy.wait_send()


BLOCK = 48


def reduce_all(grads, shards, replicas):
    layers = len(grads)
    deep = replicas // 2
    ins = []
    for layer in range(layers):
        for g in grads[layer][:4]:
            ins.append(
                g.astype(jnp.bfloat16).reshape(shards, 2, g.shape[0] // shards // 2, g.shape[1])
            )
    smalls = []
    for layer in range(layers):
        gg, gb, gu = grads[layer][4:]
        width = gg.shape[1] // shards
        smalls.append(jnp.concatenate([
            gg.reshape(-1, shards, width).transpose(1, 0, 2),
            gb.reshape(-1, shards, width).transpose(1, 0, 2),
            gu.reshape(shards, -1, width),
        ], 1))
    ng, nb = grads[0][4].shape[0], grads[0][5].shape[0]
    small = jnp.concatenate(smalls, 1)
    rows = small.shape[1]
    half = rows // 2
    small = small.reshape(shards, 2, half, width).astype(jnp.bfloat16)
    small = jnp.pad(small, ((0, 0), (0, 0), (0, -half % BLOCK), (0, -width % 128)))
    ins.append(small)
    count = len(ins)
    shapes = [x.shape for x in ins]
    total = sum(len(blocks_of(s[2:])) for s in shapes)
    per = -(-total // deep)
    sems = pltpu.SemaphoreType.DMA
    vmem = lambda *s: pltpu.VMEM(s, jnp.bfloat16)
    outs = pl.pallas_call(
        functools.partial(reduce_kernel, shards, deep, per, count),
        out_shape=[jax.ShapeDtypeStruct(s[1:], jnp.float32) for s in shapes],
        in_specs=[pl.BlockSpec(memory_space=pltpu.VMEM)] * count,
        out_specs=[pl.BlockSpec(memory_space=pltpu.VMEM)] * count,
        scratch_shapes=[vmem(s[0], *s[2:]) for s in shapes]
        + [vmem(s[0], *s[2:]) for s in shapes]
        + [vmem(s[0] - 1, *s[2:]) for s in shapes]
        + [
            vmem(deep, per, BLOCK, 128), vmem(deep - 1, per, BLOCK, 128),
            vmem(per, BLOCK, 128), vmem(deep, per, BLOCK, 128), vmem(deep, per, BLOCK, 128),
            sems((count,)), sems((count,)),
            sems((count, shards - 1)), sems((count, shards - 1)),
            sems((deep - 1,)), sems((deep - 1,)),
            sems((deep - 1,)), sems((deep - 1,)),
            sems((deep,)), sems((deep,)), sems((1,)),
        ],
        compiler_params=pltpu.CompilerParams(
            collective_id=1, has_side_effects=True, vmem_limit_bytes=56 * 1024 * 1024
        ),
        name="reduce_grads",
    )(*ins)
    big = [
        jnp.stack([outs[layer * 4 + a].reshape(-1, shapes[a][3]) for layer in range(layers)], 0)
        for a in range(4)
    ]
    tiny = outs[-1][:, :half, :width].reshape(layers, rows // layers, width)
    return tuple(big) + (
        tiny[:, :ng],
        tiny[:, ng : ng + nb],
        tiny[:, ng + nb :].reshape(layers, -1),
    )


def on_device(shards, replicas, images, cotangent, counts, *stacks):
    slot_count = images.shape[0]
    live = (jnp.arange(slot_count, dtype=jnp.int32) < counts[0]).astype(jnp.float32)[:, None, None]
    params = gather(stacks, shards)
    kept = []
    stream = images
    for layer in range(LAYERS):
        stream, saved = forward_layer(stream, params[layer])
        kept.append(saved)
    activations = stream * live
    grad = (cotangent * live).reshape(-1, D)
    grads = [None] * LAYERS
    for layer in reversed(range(LAYERS)):
        grad, grads[layer] = backward_layer(kept[layer], grad, params[layer])
    totals = reduce_all(grads, shards, replicas)
    return (activations, grad.reshape(images.shape)) + totals


def solution(mesh):
    in_specs = (
        P(("shard", "replica"), None, None),
        P(("shard", "replica"), None, None),
        P(("shard", "replica")),
        P(None, "shard", None),
        P(None, "shard", None),
        P(None, "shard", None),
        P(None, "shard", None),
        P(None, None, "shard"),
        P(None, None, "shard"),
        P(None, "shard"),
    )
    out_specs = (
        P(("shard", "replica"), None, None),
        P(("shard", "replica"), None, None),
        P(None, "shard", None),
        P(None, "shard", None),
        P(None, "shard", None),
        P(None, "shard", None),
        P(None, None, "shard"),
        P(None, None, "shard"),
        P(None, "shard"),
    )
    return jax.shard_map(
        functools.partial(on_device, mesh.shape["shard"], mesh.shape["replica"]), mesh=mesh, in_specs=in_specs, out_specs=out_specs, check_vma=False
    )
```

```python
import functools

import jax
import jax.numpy as jnp
from jax import lax
from jax.experimental import pallas as pl
from jax.experimental.pallas import tpu as pltpu
from jax.sharding import PartitionSpec as P

D = 384
HEADS = 6
HD = 64
S = 197
LAYERS = 2


EPS = 1e-06
INV_ROOT_TWO = 0.7071067811865476
INV_ROOT_TWO_PI = 0.3989422804014327


def normalize(values, gain, shift):
    center = jnp.mean(values, -1, keepdims=True)
    centered = values - center
    spread = jnp.mean(centered * centered, -1, keepdims=True)
    inverse = lax.rsqrt(spread + EPS)
    unit = centered * inverse
    return (unit * gain + shift, unit, inverse)


def norm_back(upstream, unit, inverse, gain):
    scaled = upstream * gain
    inner = (
        scaled
        - jnp.mean(scaled, -1, keepdims=True)
        - unit * jnp.mean(scaled * unit, -1, keepdims=True)
    )
    return (inverse * inner, jnp.sum(upstream * unit, 0), jnp.sum(upstream, 0))


def normal_cdf(values):
    return 0.5 * (1.0 + jax.scipy.special.erf(values * INV_ROOT_TWO))


def product(left, right):
    return jnp.dot(left, right, preferred_element_type=jnp.float32)


def product_left(left, right):
    return lax.dot_general(
        left, right, (((0,), (0,)), ((), ())), preferred_element_type=jnp.float32
    )


def product_right(left, right):
    return lax.dot_general(
        left, right, (((1,), (1,)), ((), ())), preferred_element_type=jnp.float32
    )


def batched(form, left, right):
    return jnp.einsum(form, left, right, preferred_element_type=jnp.float32)


def forward_layer(stream, params):
    w_qkv, w_out, w_up, w_down, gains, biases, up_bias = params
    gains = gains.astype(jnp.float32)
    biases = biases.astype(jnp.float32)
    up_bias = up_bias.astype(jnp.float32)
    blocks = stream.shape[0]
    factor = HD ** (-0.5)
    rows_in = stream.reshape(-1, D)
    normed_f, unit_one, scale_one = normalize(rows_in, gains[0], biases[0])
    normed_one = normed_f.astype(jnp.bfloat16)
    project = product(normed_one, w_qkv)
    queries = (
        ((project[:, :D] + biases[1]) * factor).astype(jnp.bfloat16).reshape(blocks, S, HEADS, HD)
    )
    key_rows = project[:, D : 2 * D].astype(jnp.bfloat16).reshape(blocks, S, HEADS, HD)
    values = (project[:, 2 * D :] + biases[2]).astype(jnp.bfloat16).reshape(blocks, S, HEADS, HD)
    scores = batched("bqhe,bkhe->bhqk", queries, key_rows)
    log_total = jnp.log(jnp.sum(jnp.exp(scores), -1, keepdims=True))
    probs = jnp.exp(scores - log_total)
    prob_low = probs.astype(jnp.bfloat16)
    mixed = batched("bhqk,bkhe->bqhe", prob_low, values).reshape(-1, D).astype(jnp.bfloat16)
    middle = rows_in + product(mixed, w_out) + biases[3]
    normed_g, unit_two, scale_two = normalize(middle, gains[1], biases[4])
    normed_two = normed_g.astype(jnp.bfloat16)
    hidden = product(normed_two, w_up) + up_bias
    activated = (hidden * normal_cdf(hidden)).astype(jnp.bfloat16)
    result = middle + product(activated, w_down) + biases[5]
    saved = (
        normed_one,
        unit_one,
        scale_one,
        queries,
        key_rows,
        values,
        log_total,
        mixed,
        normed_two,
        unit_two,
        scale_two,
        hidden,
        activated,
    )
    return (result.reshape(stream.shape), saved)


def backward_layer(saved, grad, params):
    w_qkv, w_out, w_up, w_down, gains, biases, up_bias = params
    gains_f = gains.astype(jnp.float32)
    factor = HD ** (-0.5)
    (
        normed_one,
        unit_one,
        scale_one,
        queries,
        key_rows,
        values,
        log_total,
        mixed,
        normed_two,
        unit_two,
        scale_two,
        hidden,
        activated,
    ) = saved
    blocks = queries.shape[0]
    low = grad.astype(jnp.bfloat16)
    down_grad = product_left(activated, low)
    shift_five = jnp.sum(grad, 0)
    act_grad = product_right(low, w_down)
    dens = jnp.exp(-0.5 * hidden * hidden) * INV_ROOT_TWO_PI
    hid_grad = act_grad * (normal_cdf(hidden) + hidden * dens)
    hid_low = hid_grad.astype(jnp.bfloat16)
    up_grad = product_left(normed_two, hid_low)
    upbias_grad = jnp.sum(hid_grad, 0)
    norm_grad = product_right(hid_low, w_up)
    back_two, gain_two, shift_four = norm_back(norm_grad, unit_two, scale_two, gains_f[1])
    mid_grad = grad + back_two
    mid_low = mid_grad.astype(jnp.bfloat16)
    out_grad = product_left(mixed, mid_low)
    shift_three = jnp.sum(mid_grad, 0)
    mixed_grad = product_right(mid_low, w_out).astype(jnp.bfloat16).reshape(blocks, S, HEADS, HD)
    scores = batched("bqhe,bkhe->bhqk", queries, key_rows)
    probs = jnp.exp(scores - log_total)
    prob_low = probs.astype(jnp.bfloat16)
    prob_grad = batched("bqhe,bkhe->bhqk", mixed_grad, values)
    row_dot = jnp.sum(probs * prob_grad, -1, keepdims=True)
    score_grad = (probs * (prob_grad - row_dot)).astype(jnp.bfloat16)
    query_grad = (batched("bhqk,bkhe->bqhe", score_grad, key_rows) * factor).reshape(-1, D)
    key_grad = batched("bhqk,bqhe->bkhe", score_grad, queries).reshape(-1, D)
    value_grad = batched("bhqk,bqhe->bkhe", prob_low, mixed_grad).reshape(-1, D)
    project_grad = jnp.concatenate([query_grad, key_grad, value_grad], 1).astype(jnp.bfloat16)
    qkv_grad = product_left(normed_one, project_grad)
    first_grad = product_right(project_grad, w_qkv)
    back_one, gain_one, shift_zero = norm_back(first_grad, unit_one, scale_one, gains_f[0])
    stream_grad = mid_grad + back_one
    grads = (
        qkv_grad,
        out_grad,
        up_grad,
        down_grad,
        jnp.stack([gain_one, gain_two], 0),
        jnp.stack(
            [
                shift_zero,
                jnp.sum(query_grad, 0),
                jnp.sum(value_grad, 0),
                shift_three,
                shift_four,
                shift_five,
            ],
            0,
        ),
        upbias_grad,
    )
    return (stream_grad, grads)


MESH = pl.DeviceIdType.MESH


def place(shards, replicas):
    me = lax.axis_index("shard")
    rep = lax.axis_index("replica")
    core = lax.rem(rep, 2)
    depth = lax.div(rep, 2)
    return me, rep, core, depth, rep + 1 - 2 * core


def gather_kernel(shards, layers, count, *refs):
    ins = refs[: count + 1]
    outs = refs[count + 1 : count + 2 + count * layers]
    send, recv, psend, precv, ssend, srecv, local = refs[count + 2 + count * layers :]
    me, rep, core, depth, mate = place(shards, 0)
    barrier = pltpu.get_barrier_semaphore()
    pl.semaphore_signal(barrier, inc=1, device_id=(me, mate), device_id_type=MESH)
    for k in range(1, shards):
        peer = lax.rem(me + k, shards)
        pl.semaphore_signal(barrier, inc=1, device_id=(peer, rep), device_id_type=MESH)
    pl.semaphore_wait(barrier, shards)
    small_in, small_out = ins[count], outs[count * layers]
    smalls = []
    for k in range(1, shards):
        peer = lax.rem(me + k, shards)
        copy = pltpu.make_async_remote_copy(
            src_ref=small_in, dst_ref=small_out.at[me], send_sem=ssend.at[k - 1],
            recv_sem=srecv.at[k - 1], device_id=(peer, rep), device_id_type=MESH)
        copy.start()
        smalls.append(copy)
    side = (me + 1 - 2 * lax.rem(me, 2), lax.rem(me + 2, shards))
    items = layers * count
    first = []
    for layer in range(layers):
        for a in range(count):
            item = layer * count + a
            for k in range(2):
                copy = pltpu.make_async_remote_copy(
                    src_ref=ins[a].at[layer, core], dst_ref=outs[item].at[me, core],
                    send_sem=send.at[item, k], recv_sem=recv.at[item, k],
                    device_id=(side[k], rep), device_id_type=MESH)
                copy.start()
                first.append(copy)
    own = []
    for layer in range(layers):
        for a in range(count):
            item = layer * count + a
            copy = pltpu.make_async_copy(ins[a].at[layer], outs[item].at[me], local.at[item])
            copy.start()
            own.append(copy)
    copy = pltpu.make_async_copy(small_in, small_out.at[me], local.at[layers * count])
    copy.start()
    own.append(copy)
    second = []

    def to_mate(item, slot, origin):
        piece = outs[item].at[origin, core]
        passed = pltpu.make_async_remote_copy(
            src_ref=piece, dst_ref=piece, send_sem=psend.at[item, slot],
            recv_sem=precv.at[item, slot], device_id=(me, mate), device_id_type=MESH)
        passed.start()
        second.append(passed)

    relays = [None] * items
    for item in range(items + 1):
        if item < items:
            via = (item + item // count) % 2
            for k in (via, 1 - via):
                first[2 * item + k].wait_recv()
                if k == via:
                    piece = outs[item].at[side[via], core]
                    relays[item] = pltpu.make_async_remote_copy(
                        src_ref=piece, dst_ref=piece, send_sem=send.at[item, 2],
                        recv_sem=recv.at[item, 2], device_id=(side[1 - via], rep),
                        device_id_type=MESH)
                    relays[item].start()
                to_mate(item, k, side[k])
        if item > 0:
            relays[item - 1].wait_recv()
            to_mate(item - 1, 2, shards - 1 - me)
    for copy in smalls:
        copy.wait()
    for copy in own:
        copy.wait()
    for copy in first + relays:
        copy.wait_send()
    for copy in second:
        copy.wait()


def gather(stacks, shards):
    weights = stacks[:4]
    layers = weights[0].shape[0]
    ins = [w.reshape(layers, 2, w.shape[1] // 2, w.shape[2]) for w in weights]
    gains, biases, up_bias = stacks[4:]
    width = gains.shape[2]
    small = jnp.concatenate([gains, biases, up_bias.reshape(layers, -1, width)], 1)
    rows = small.shape[1]
    small = jnp.pad(small, ((0, 0), (0, -rows % 16), (0, -width % 128)))
    count = len(ins)
    shapes = [
        jax.ShapeDtypeStruct((shards,) + w.shape[1:], w.dtype) for _ in range(layers) for w in ins
    ]
    shapes.append(jax.ShapeDtypeStruct((shards,) + small.shape, small.dtype))
    sems = pltpu.SemaphoreType.DMA
    items = layers * count
    outs = pl.pallas_call(
        functools.partial(gather_kernel, shards, layers, count),
        out_shape=shapes,
        in_specs=[pl.BlockSpec(memory_space=pltpu.VMEM)] * (count + 1),
        out_specs=[pl.BlockSpec(memory_space=pl.ANY)] * len(shapes),
        scratch_shapes=[
            sems((items, shards - 1)), sems((items, shards - 1)),
            sems((items, shards - 1)), sems((items, shards - 1)),
            sems((shards - 1,)), sems((shards - 1,)), sems((items + 1,)),
        ],
        compiler_params=pltpu.CompilerParams(collective_id=0, has_side_effects=True),
        name="gather_params",
    )(*ins, small)
    tiny = outs[-1][:, :, :rows, :width]
    params = []
    for layer in range(layers):
        big = [outs[layer * count + a].reshape(-1, weights[a].shape[2]) for a in range(count)]
        part = tiny[:, layer]
        ng, nb = gains.shape[1], biases.shape[1]
        params.append(tuple(big) + (
            part[:, :ng].transpose(1, 0, 2).reshape(ng, -1),
            part[:, ng : ng + nb].transpose(1, 0, 2).reshape(nb, -1),
            part[:, ng + nb :].reshape(-1),
        ))
    return params


BLOCK = 48


def blocks_of(shape):
    return [(r, c) for r in range(shape[0] // BLOCK) for c in range(shape[1] // 128)]


def reduce_kernel(shards, deep, plan, groups, pers, turn, *refs):
    count = len(plan)
    kinds = 1 + max(kind for kind, _, _ in plan)
    many = len(groups)
    ins, outs = refs[:count], refs[count : count + kinds]
    refs = refs[count + kinds :]
    buf_a, buf_s, buf_b = refs[:count], refs[count : 2 * count], refs[2 * count : 3 * count]
    z_own, z_recv, z_sum, z_all, z_mate = [
        refs[3 * count + n * many : 3 * count + (n + 1) * many] for n in range(5)
    ]
    a_send, a_recv, b_send, b_recv, c_send, c_recv, d_send, d_recv, e_send, e_recv, loc = refs[
        3 * count + 5 * many :
    ]
    me, rep, core, depth, mate = place(shards, deep)
    side = (me + 1 - 2 * lax.rem(me, 2), lax.rem(me + 2, shards))
    far = shards - 1 - me
    barrier = pltpu.get_barrier_semaphore()
    pl.semaphore_signal(barrier, inc=1, device_id=(me, mate), device_id_type=MESH)
    for k in range(2):
        pl.semaphore_signal(barrier, inc=1, device_id=(side[k], rep), device_id_type=MESH)
    for k in range(1, deep):
        peer = lax.rem(depth + k, deep) * 2 + core
        pl.semaphore_signal(barrier, inc=1, device_id=(me, peer), device_id_type=MESH)
    pl.semaphore_wait(barrier, deep + 2)

    def wide(value):
        return value.astype(jnp.float32)

    def remote(src, dst, send, recv, device):
        copy = pltpu.make_async_remote_copy(
            src_ref=src, dst_ref=dst, send_sem=send, recv_sem=recv, device_id=device,
            device_id_type=MESH)
        copy.start()
        return copy

    stage_a = {}
    for group in groups:
        for a in group:
            stage_a[a] = remote(
                ins[a].at[:, 1 - core], buf_a[a], a_send.at[a], a_recv.at[a], (me, mate))
    one, two, stage_c, stage_d, stage_e = {}, {}, {}, {}, {}

    def pair(a, dest):
        return wide(ins[a][dest, core]) + wide(buf_a[a][dest])

    def do_one(g):
        for a in groups[g]:
            stage_a[a].wait_recv()
            near = side[turn[a]]
            buf_s[a][0] = pair(a, near).astype(jnp.bfloat16)
            buf_s[a][1] = pair(a, far).astype(jnp.bfloat16)
            one[a] = remote(
                buf_s[a].at[pl.ds(0, 2)], buf_b[a].at[pl.ds(0, 2)], b_send.at[a, 0],
                b_recv.at[a, 0], (near, rep))

    def do_two(g):
        for a in groups[g]:
            one[a].wait_recv()
            near = side[1 - turn[a]]
            buf_s[a][2] = (pair(a, near) + wide(buf_b[a][1])).astype(jnp.bfloat16)
            two[a] = remote(
                buf_s[a].at[2], buf_b[a].at[2], b_send.at[a, 1], b_recv.at[a, 1], (near, rep))

    def do_scatter(g):
        per, number = pers[g], 0
        for a in groups[g]:
            two[a].wait_recv()
            for r, c in blocks_of(buf_a[a].shape[1:]):
                rows, cols = pl.ds(r * BLOCK, BLOCK), pl.ds(c * 128, 128)
                total = wide(ins[a][me, core, rows, cols]) + wide(buf_a[a][me, rows, cols])
                total = total + wide(buf_b[a][0, rows, cols]) + wide(buf_b[a][2, rows, cols])
                z_own[g][number // per, number % per] = total.astype(jnp.bfloat16)
                number += 1
        while number < deep * per:
            z_own[g][number // per, number % per] = jnp.zeros((BLOCK, 128), jnp.bfloat16)
            number += 1
        stage_c[g] = []
        for k in range(1, deep):
            peer = lax.rem(depth + k, deep)
            stage_c[g].append(remote(
                z_own[g].at[peer], z_recv[g].at[k - 1], c_send.at[g, k - 1],
                c_recv.at[g, k - 1], (me, peer * 2 + core)))

    def do_spread(g):
        for copy in stage_c[g]:
            copy.wait_recv()
        for b in range(pers[g]):
            total = wide(z_own[g][depth, b])
            for k in range(deep - 1):
                total = total + wide(z_recv[g][k, b])
            z_sum[g][b] = total.astype(jnp.bfloat16)
        stage_d[g] = []
        for k in range(1, deep):
            peer = lax.rem(depth + k, deep)
            stage_d[g].append(remote(
                z_sum[g], z_all[g].at[depth], d_send.at[g, k - 1], d_recv.at[g, k - 1],
                (me, peer * 2 + core)))
        own = pltpu.make_async_copy(z_sum[g], z_all[g].at[depth], loc.at[g])
        own.start()
        own.wait()

    def do_swap(g):
        for copy in stage_d[g]:
            copy.wait_recv()
        stage_e[g] = remote(z_all[g], z_mate[g], e_send.at[g], e_recv.at[g], (me, mate))
        put(g, z_all[g], core)

    def do_last(g):
        stage_e[g].wait_recv()
        put(g, z_mate[g], 1 - core)

    def put(g, held, half):
        per, at = pers[g], 0
        for a in groups[g]:
            kind, layer, start = plan[a]
            for r, c in blocks_of(buf_a[a].shape[1:]):
                rows, cols = pl.ds(r * BLOCK, BLOCK), pl.ds(start + c * 128, 128)
                outs[kind][layer, half, rows, cols] = wide(held[at // per, at % per])
                at += 1

    stages = (do_one, do_two, do_scatter, do_spread, do_swap, do_last)
    for t in range(many + len(stages) - 1):
        for n, stage in enumerate(stages):
            if 0 <= t - n < many:
                stage(t - n)
    for group in (stage_a, one, two, stage_e):
        for copy in group.values():
            copy.wait_send()
    for group in (stage_c, stage_d):
        for copies in group.values():
            for copy in copies:
                copy.wait_send()


def reduce_all(grads, shards, replicas):
    layers = len(grads)
    deep = replicas // 2
    ins, plan, groups = [], [], []
    for layer in reversed(range(layers)):
        qkv, out, up, down = grads[layer][:4]
        cut = (qkv.shape[1] + out.shape[1]) // 2
        order = [[(3, down, 0), (2, up, 0)], [(0, qkv[:, :cut], 0), (0, qkv[:, cut:], cut), (1, out, 0)]]
        for part in order:
            group = []
            for kind, g, start in part:
                group.append(len(ins))
                plan.append((kind, layer, start))
                ins.append(
                    g.astype(jnp.bfloat16).reshape(shards, 2, g.shape[0] // shards // 2, g.shape[1])
                )
            if len(group) == 3:
                group = [group[0], group[1], None, group[2]]
            groups.append(group)
    smalls = []
    for layer in range(layers):
        gg, gb, gu = grads[layer][4:]
        width = gg.shape[1] // shards
        smalls.append(jnp.concatenate([
            gg.reshape(-1, shards, width).transpose(1, 0, 2),
            gb.reshape(-1, shards, width).transpose(1, 0, 2),
            gu.reshape(shards, -1, width),
        ], 1))
    ng, nb = grads[0][4].shape[0], grads[0][5].shape[0]
    small = jnp.concatenate(smalls, 1)
    rows = small.shape[1]
    half = rows // 2
    small = small.reshape(shards, 2, half, width).astype(jnp.bfloat16)
    small = jnp.pad(small, ((0, 0), (0, 0), (0, -half % BLOCK), (0, -width % 128)))
    groups[-1].append(len(ins))
    plan.append((4, 0, 0))
    ins.append(small)
    count = len(ins)
    turns = [None] * count
    for group in groups:
        for n, a in enumerate(group):
            if a is not None:
                turns[a] = n % 2
    groups = [[a for a in group if a is not None] for group in groups]
    shapes = [x.shape for x in ins]
    pers = [-(-sum(len(blocks_of(shapes[a][2:])) for a in group) // deep) for group in groups]
    many = len(groups)
    sems = pltpu.SemaphoreType.DMA
    vmem = lambda *s: pltpu.VMEM(s, jnp.bfloat16)
    out_shapes = [
        (layers, 2, g.shape[0] // shards // 2, g.shape[1]) for g in grads[0][:4]
    ] + [(1,) + shapes[-1][1:]]
    outs = pl.pallas_call(
        functools.partial(reduce_kernel, shards, deep, plan, groups, pers, turns),
        out_shape=[jax.ShapeDtypeStruct(s, jnp.float32) for s in out_shapes],
        in_specs=[pl.BlockSpec(memory_space=pltpu.VMEM)] * count,
        out_specs=[pl.BlockSpec(memory_space=pltpu.VMEM)] * len(out_shapes),
        scratch_shapes=[vmem(s[0], *s[2:]) for s in shapes]
        + [vmem(3, *s[2:]) for s in shapes]
        + [vmem(3, *s[2:]) for s in shapes]
        + [vmem(deep, per, BLOCK, 128) for per in pers]
        + [vmem(deep - 1, per, BLOCK, 128) for per in pers]
        + [vmem(per, BLOCK, 128) for per in pers]
        + [vmem(deep, per, BLOCK, 128) for per in pers]
        + [vmem(deep, per, BLOCK, 128) for per in pers]
        + [
            sems((count,)), sems((count,)),
            sems((count, 2)), sems((count, 2)),
            sems((many, deep - 1)), sems((many, deep - 1)),
            sems((many, deep - 1)), sems((many, deep - 1)),
            sems((many,)), sems((many,)), sems((many,)),
        ],
        compiler_params=pltpu.CompilerParams(
            collective_id=1, has_side_effects=True, vmem_limit_bytes=56 * 1024 * 1024
        ),
        name="reduce_grads",
    )(*ins)
    big = [x.reshape(layers, -1, x.shape[3]) for x in outs[:4]]
    tiny = outs[-1][0, :, :half, :width].reshape(layers, rows // layers, width)
    return tuple(big) + (
        tiny[:, :ng],
        tiny[:, ng : ng + nb],
        tiny[:, ng + nb :].reshape(layers, -1),
    )


def on_device(shards, replicas, images, cotangent, counts, *stacks):
    slot_count = images.shape[0]
    live = (jnp.arange(slot_count, dtype=jnp.int32) < counts[0]).astype(jnp.float32)[:, None, None]
    params = gather(stacks, shards)
    kept = []
    stream = images
    for layer in range(LAYERS):
        stream, saved = forward_layer(stream, params[layer])
        kept.append(saved)
    activations = stream * live
    grad = (cotangent * live).reshape(-1, D)
    grads = [None] * LAYERS
    for layer in reversed(range(LAYERS)):
        grad, grads[layer] = backward_layer(kept[layer], grad, params[layer])
    totals = reduce_all(grads, shards, replicas)
    return (activations, grad.reshape(images.shape)) + totals


def solution(mesh):
    in_specs = (
        P(("shard", "replica"), None, None),
        P(("shard", "replica"), None, None),
        P(("shard", "replica")),
        P(None, "shard", None),
        P(None, "shard", None),
        P(None, "shard", None),
        P(None, "shard", None),
        P(None, None, "shard"),
        P(None, None, "shard"),
        P(None, "shard"),
    )
    out_specs = (
        P(("shard", "replica"), None, None),
        P(("shard", "replica"), None, None),
        P(None, "shard", None),
        P(None, "shard", None),
        P(None, "shard", None),
        P(None, "shard", None),
        P(None, None, "shard"),
        P(None, None, "shard"),
        P(None, "shard"),
    )
    return jax.shard_map(
        functools.partial(on_device, mesh.shape["shard"], mesh.shape["replica"]), mesh=mesh, in_specs=in_specs, out_specs=out_specs, check_vma=False
    )
```

```python
import functools

import jax
import jax.numpy as jnp
from jax import lax
from jax.experimental import pallas as pl
from jax.experimental.pallas import tpu as pltpu
from jax.sharding import PartitionSpec as P

D = 384
HEADS = 6
HD = 64
S = 197
LAYERS = 2


EPS = 1e-06
INV_ROOT_TWO = 0.7071067811865476
INV_ROOT_TWO_PI = 0.3989422804014327


def normalize(values, gain, shift):
    center = jnp.mean(values, -1, keepdims=True)
    centered = values - center
    spread = jnp.mean(centered * centered, -1, keepdims=True)
    inverse = lax.rsqrt(spread + EPS)
    unit = centered * inverse
    return (unit * gain + shift, unit, inverse)


def norm_back(upstream, unit, inverse, gain):
    scaled = upstream * gain
    inner = (
        scaled
        - jnp.mean(scaled, -1, keepdims=True)
        - unit * jnp.mean(scaled * unit, -1, keepdims=True)
    )
    return (inverse * inner, jnp.sum(upstream * unit, 0), jnp.sum(upstream, 0))


def normal_cdf(values):
    return 0.5 * (1.0 + jax.scipy.special.erf(values * INV_ROOT_TWO))


def product(left, right):
    return jnp.dot(left, right, preferred_element_type=jnp.float32)


def product_left(left, right):
    return lax.dot_general(
        left, right, (((0,), (0,)), ((), ())), preferred_element_type=jnp.float32
    )


def product_right(left, right):
    return lax.dot_general(
        left, right, (((1,), (1,)), ((), ())), preferred_element_type=jnp.float32
    )


def batched(form, left, right):
    return jnp.einsum(form, left, right, preferred_element_type=jnp.float32)


def forward_layer(stream, params):
    w_qkv, w_out, w_up, w_down, gains, biases, up_bias = params
    gains = gains.astype(jnp.float32)
    biases = biases.astype(jnp.float32)
    up_bias = up_bias.astype(jnp.float32)
    blocks = stream.shape[0]
    factor = HD ** (-0.5)
    rows_in = stream.reshape(-1, D)
    normed_f, unit_one, scale_one = normalize(rows_in, gains[0], biases[0])
    normed_one = normed_f.astype(jnp.bfloat16)
    project = product(normed_one, w_qkv)
    queries = (
        ((project[:, :D] + biases[1]) * factor).astype(jnp.bfloat16).reshape(blocks, S, HEADS, HD)
    )
    key_rows = project[:, D : 2 * D].astype(jnp.bfloat16).reshape(blocks, S, HEADS, HD)
    values = (project[:, 2 * D :] + biases[2]).astype(jnp.bfloat16).reshape(blocks, S, HEADS, HD)
    scores = batched("bqhe,bkhe->bhqk", queries, key_rows)
    log_total = jnp.log(jnp.sum(jnp.exp(scores), -1, keepdims=True))
    probs = jnp.exp(scores - log_total)
    prob_low = probs.astype(jnp.bfloat16)
    mixed = batched("bhqk,bkhe->bqhe", prob_low, values).reshape(-1, D).astype(jnp.bfloat16)
    middle = rows_in + product(mixed, w_out) + biases[3]
    normed_g, unit_two, scale_two = normalize(middle, gains[1], biases[4])
    normed_two = normed_g.astype(jnp.bfloat16)
    hidden = product(normed_two, w_up) + up_bias
    activated = (hidden * normal_cdf(hidden)).astype(jnp.bfloat16)
    result = middle + product(activated, w_down) + biases[5]
    saved = (
        normed_one,
        unit_one,
        scale_one,
        queries,
        key_rows,
        values,
        log_total,
        mixed,
        normed_two,
        unit_two,
        scale_two,
        hidden,
        activated,
    )
    return (result.reshape(stream.shape), saved)


def backward_layer(saved, grad, params):
    w_qkv, w_out, w_up, w_down, gains, biases, up_bias = params
    gains_f = gains.astype(jnp.float32)
    factor = HD ** (-0.5)
    (
        normed_one,
        unit_one,
        scale_one,
        queries,
        key_rows,
        values,
        log_total,
        mixed,
        normed_two,
        unit_two,
        scale_two,
        hidden,
        activated,
    ) = saved
    blocks = queries.shape[0]
    low = grad.astype(jnp.bfloat16)
    down_grad = product_left(activated, low)
    shift_five = jnp.sum(grad, 0)
    act_grad = product_right(low, w_down)
    dens = jnp.exp(-0.5 * hidden * hidden) * INV_ROOT_TWO_PI
    hid_grad = act_grad * (normal_cdf(hidden) + hidden * dens)
    hid_low = hid_grad.astype(jnp.bfloat16)
    up_grad = product_left(normed_two, hid_low)
    upbias_grad = jnp.sum(hid_grad, 0)
    norm_grad = product_right(hid_low, w_up)
    back_two, gain_two, shift_four = norm_back(norm_grad, unit_two, scale_two, gains_f[1])
    mid_grad = grad + back_two
    mid_low = mid_grad.astype(jnp.bfloat16)
    out_grad = product_left(mixed, mid_low)
    shift_three = jnp.sum(mid_grad, 0)
    mixed_grad = product_right(mid_low, w_out).astype(jnp.bfloat16).reshape(blocks, S, HEADS, HD)
    scores = batched("bqhe,bkhe->bhqk", queries, key_rows)
    probs = jnp.exp(scores - log_total)
    prob_low = probs.astype(jnp.bfloat16)
    prob_grad = batched("bqhe,bkhe->bhqk", mixed_grad, values)
    row_dot = jnp.sum(probs * prob_grad, -1, keepdims=True)
    score_grad = (probs * (prob_grad - row_dot)).astype(jnp.bfloat16)
    query_grad = (batched("bhqk,bkhe->bqhe", score_grad, key_rows) * factor).reshape(-1, D)
    key_grad = batched("bhqk,bqhe->bkhe", score_grad, queries).reshape(-1, D)
    value_grad = batched("bhqk,bqhe->bkhe", prob_low, mixed_grad).reshape(-1, D)
    project_grad = jnp.concatenate([query_grad, key_grad, value_grad], 1).astype(jnp.bfloat16)
    qkv_grad = product_left(normed_one, project_grad)
    first_grad = product_right(project_grad, w_qkv)
    back_one, gain_one, shift_zero = norm_back(first_grad, unit_one, scale_one, gains_f[0])
    stream_grad = mid_grad + back_one
    grads = (
        qkv_grad,
        out_grad,
        up_grad,
        down_grad,
        jnp.stack([gain_one, gain_two], 0),
        jnp.stack(
            [
                shift_zero,
                jnp.sum(query_grad, 0),
                jnp.sum(value_grad, 0),
                shift_three,
                shift_four,
                shift_five,
            ],
            0,
        ),
        upbias_grad,
    )
    return (stream_grad, grads)


MESH = pl.DeviceIdType.MESH


def place(shards, replicas):
    me = lax.axis_index("shard")
    rep = lax.axis_index("replica")
    core = lax.rem(rep, 2)
    depth = lax.div(rep, 2)
    return me, rep, core, depth, rep + 1 - 2 * core


def gather_kernel(shards, layers, count, *refs):
    ins, outs = refs[: count + 1], refs[count + 1 : 2 * count + 2]
    send, recv, psend, precv, zsend, zrecv, qsend, qrecv, ssend, srecv, local = refs[2 * count + 2 :]
    me, rep, core, depth, mate = place(shards, 0)
    odd = lax.rem(depth, 2)
    across = (depth + 1 - 2 * odd) * 2 + core
    side = (me + 1 - 2 * lax.rem(me, 2), lax.rem(me + 2, shards))
    far = shards - 1 - me
    barrier = pltpu.get_barrier_semaphore()
    pl.semaphore_signal(barrier, inc=1, device_id=(me, mate), device_id_type=MESH)
    pl.semaphore_signal(barrier, inc=1, device_id=(me, across), device_id_type=MESH)
    for k in range(1, shards):
        peer = lax.rem(me + k, shards)
        pl.semaphore_signal(barrier, inc=1, device_id=(peer, rep), device_id_type=MESH)
    pl.semaphore_wait(barrier, shards + 1)

    started = []

    def remote(src, dst, send_sem, recv_sem, device):
        copy = pltpu.make_async_remote_copy(
            src_ref=src, dst_ref=dst, send_sem=send_sem, recv_sem=recv_sem, device_id=device,
            device_id_type=MESH)
        copy.start()
        started.append(copy)
        return copy

    small_in, small_out = ins[count], outs[count]
    swapped = [(a, odd) for a in (2, 0, 1)]
    items = swapped + [(3, layer) for layer in range(layers)]
    first = []
    for item, (a, layer) in enumerate(items):
        for k in range(2):
            first.append(remote(
                ins[a].at[layer, core], outs[a].at[layer, me, core], send.at[item, k],
                recv.at[item, k], (side[k], rep)))
    smalls = []
    for k in range(1, shards):
        peer = lax.rem(me + k, shards)
        smalls.append(remote(
            small_in, small_out.at[me], ssend.at[k - 1], srecv.at[k - 1], (peer, rep)))
    own = []
    for a in range(count):
        for layer in range(layers):
            copy = pltpu.make_async_copy(
                ins[a].at[layer], outs[a].at[layer, me], local.at[a * layers + layer])
            copy.start()
            own.append(copy)
    copy = pltpu.make_async_copy(small_in, small_out.at[me], local.at[layers * count])
    copy.start()
    own.append(copy)
    passed, crossed = [], []

    def hand_on(item, slot, origin):
        a, layer = items[item]
        piece = outs[a].at[layer, origin, core]
        if item < len(swapped):
            copy = remote(piece, piece, zsend.at[item, slot], zrecv.at[item, slot], (me, across))
            crossed.append((item, slot, origin, copy))
        passed.append(
            remote(piece, piece, psend.at[item, slot], precv.at[item, slot], (me, mate)))

    relays = []
    for item in range(len(items) + 1):
        if item < len(items):
            a, layer = items[item]
            via = item % 2
            for k in (via, 1 - via):
                first[2 * item + k].wait_recv()
                if k == via:
                    piece = outs[a].at[layer, side[via], core]
                    relays.append(remote(
                        piece, piece, send.at[item, 2], recv.at[item, 2], (side[1 - via], rep)))
                hand_on(item, k, side[k])
        if item > 0:
            relays[item - 1].wait_recv()
            hand_on(item - 1, 2, far)
    for item, slot, origin, copy in crossed:
        copy.wait_recv()
        piece = outs[items[item][0]].at[1 - odd, origin, core]
        passed.append(
            remote(piece, piece, qsend.at[item, slot], qrecv.at[item, slot], (me, mate)))
    for copy in smalls + passed:
        copy.wait_recv()
    for copy in own:
        copy.wait()
    for copy in started:
        copy.wait_send()


def gather(stacks, shards):
    weights = stacks[:4]
    layers = weights[0].shape[0]
    ins = [w.reshape(layers, 2, w.shape[1] // 2, w.shape[2]) for w in weights]
    gains, biases, up_bias = stacks[4:]
    width = gains.shape[2]
    small = jnp.concatenate([gains, biases, up_bias.reshape(layers, -1, width)], 1)
    rows = small.shape[1]
    small = jnp.pad(small, ((0, 0), (0, -rows % 16), (0, -width % 128)))
    count = len(ins)
    shapes = [jax.ShapeDtypeStruct((layers, shards) + w.shape[1:], w.dtype) for w in ins]
    shapes.append(jax.ShapeDtypeStruct((shards,) + small.shape, small.dtype))
    sems = pltpu.SemaphoreType.DMA
    table = sems((count - 1 + layers, shards - 1))
    cross = sems((count - 1, shards - 1))
    outs = pl.pallas_call(
        functools.partial(gather_kernel, shards, layers, count),
        out_shape=shapes,
        in_specs=[pl.BlockSpec(memory_space=pltpu.VMEM)] * (count + 1),
        out_specs=[pl.BlockSpec(memory_space=pl.ANY)] * len(shapes),
        scratch_shapes=[table] * 4 + [cross] * 4
        + [sems((shards - 1,)), sems((shards - 1,)), sems((layers * count + 1,))],
        compiler_params=pltpu.CompilerParams(collective_id=0, has_side_effects=True),
        name="gather_params",
    )(*ins, small)
    tiny = outs[-1][:, :, :rows, :width]
    params = []
    for layer in range(layers):
        big = [outs[a][layer].reshape(-1, weights[a].shape[2]) for a in range(count)]
        part = tiny[:, layer]
        ng, nb = gains.shape[1], biases.shape[1]
        params.append(tuple(big) + (
            part[:, :ng].transpose(1, 0, 2).reshape(ng, -1),
            part[:, ng : ng + nb].transpose(1, 0, 2).reshape(nb, -1),
            part[:, ng + nb :].reshape(-1),
        ))
    return params


BLOCK = 48


def blocks_of(shape):
    return [(r, c) for r in range(shape[0] // BLOCK) for c in range(shape[1] // 128)]


def reduce_kernel(shards, deep, plan, groups, pers, turn, *refs):
    count = len(plan)
    kinds = 1 + max(kind for kind, _, _ in plan)
    many = len(groups)
    ins, outs = refs[:count], refs[count : count + kinds]
    refs = refs[count + kinds :]
    buf_a, buf_s, buf_b = refs[:count], refs[count : 2 * count], refs[2 * count : 3 * count]
    z_own, z_recv, z_sum, z_all, z_mate = [
        refs[3 * count + n * many : 3 * count + (n + 1) * many] for n in range(5)
    ]
    a_send, a_recv, b_send, b_recv, c_send, c_recv, d_send, d_recv, e_send, e_recv, loc = refs[
        3 * count + 5 * many :
    ]
    me, rep, core, depth, mate = place(shards, deep)
    side = (me + 1 - 2 * lax.rem(me, 2), lax.rem(me + 2, shards))
    far = shards - 1 - me
    barrier = pltpu.get_barrier_semaphore()
    pl.semaphore_signal(barrier, inc=1, device_id=(me, mate), device_id_type=MESH)
    for k in range(2):
        pl.semaphore_signal(barrier, inc=1, device_id=(side[k], rep), device_id_type=MESH)
    for k in range(1, deep):
        peer = lax.rem(depth + k, deep) * 2 + core
        pl.semaphore_signal(barrier, inc=1, device_id=(me, peer), device_id_type=MESH)
    pl.semaphore_wait(barrier, deep + 2)

    def wide(value):
        return value.astype(jnp.float32)

    def remote(src, dst, send, recv, device):
        copy = pltpu.make_async_remote_copy(
            src_ref=src, dst_ref=dst, send_sem=send, recv_sem=recv, device_id=device,
            device_id_type=MESH)
        copy.start()
        return copy

    stage_a = {}
    for group in groups:
        for a in group:
            stage_a[a] = remote(
                ins[a].at[:, 1 - core], buf_a[a], a_send.at[a], a_recv.at[a], (me, mate))
    one, two, stage_c, stage_d, stage_e = {}, {}, {}, {}, {}

    def pair(a, dest):
        return wide(ins[a][dest, core]) + wide(buf_a[a][dest])

    def do_one(g):
        for a in groups[g]:
            stage_a[a].wait_recv()
            near = side[turn[a]]
            buf_s[a][0] = pair(a, near).astype(jnp.bfloat16)
            buf_s[a][1] = pair(a, far).astype(jnp.bfloat16)
            one[a] = remote(
                buf_s[a].at[pl.ds(0, 2)], buf_b[a].at[pl.ds(0, 2)], b_send.at[a, 0],
                b_recv.at[a, 0], (near, rep))

    def do_two(g):
        for a in groups[g]:
            one[a].wait_recv()
            near = side[1 - turn[a]]
            buf_s[a][2] = (pair(a, near) + wide(buf_b[a][1])).astype(jnp.bfloat16)
            two[a] = remote(
                buf_s[a].at[2], buf_b[a].at[2], b_send.at[a, 1], b_recv.at[a, 1], (near, rep))

    def do_scatter(g):
        per, number = pers[g], 0
        for a in groups[g]:
            two[a].wait_recv()
            for r, c in blocks_of(buf_a[a].shape[1:]):
                rows, cols = pl.ds(r * BLOCK, BLOCK), pl.ds(c * 128, 128)
                total = wide(ins[a][me, core, rows, cols]) + wide(buf_a[a][me, rows, cols])
                total = total + wide(buf_b[a][0, rows, cols]) + wide(buf_b[a][2, rows, cols])
                z_own[g][number // per, number % per] = total.astype(jnp.bfloat16)
                number += 1
        while number < deep * per:
            z_own[g][number // per, number % per] = jnp.zeros((BLOCK, 128), jnp.bfloat16)
            number += 1
        stage_c[g] = []
        for k in range(1, deep):
            peer = lax.rem(depth + k, deep)
            stage_c[g].append(remote(
                z_own[g].at[peer], z_recv[g].at[k - 1], c_send.at[g, k - 1],
                c_recv.at[g, k - 1], (me, peer * 2 + core)))

    def do_spread(g):
        for copy in stage_c[g]:
            copy.wait_recv()
        for b in range(pers[g]):
            total = wide(z_own[g][depth, b])
            for k in range(deep - 1):
                total = total + wide(z_recv[g][k, b])
            z_sum[g][b] = total.astype(jnp.bfloat16)
        stage_d[g] = []
        for k in range(1, deep):
            peer = lax.rem(depth + k, deep)
            stage_d[g].append(remote(
                z_sum[g], z_all[g].at[depth], d_send.at[g, k - 1], d_recv.at[g, k - 1],
                (me, peer * 2 + core)))
        own = pltpu.make_async_copy(z_sum[g], z_all[g].at[depth], loc.at[g])
        own.start()
        own.wait()

    def do_swap(g):
        for copy in stage_d[g]:
            copy.wait_recv()
        stage_e[g] = remote(z_all[g], z_mate[g], e_send.at[g], e_recv.at[g], (me, mate))
        put(g, z_all[g], core)

    def do_last(g):
        stage_e[g].wait_recv()
        put(g, z_mate[g], 1 - core)

    def put(g, held, half):
        per, at = pers[g], 0
        for a in groups[g]:
            kind, layer, start = plan[a]
            for r, c in blocks_of(buf_a[a].shape[1:]):
                rows, cols = pl.ds(r * BLOCK, BLOCK), pl.ds(start + c * 128, 128)
                outs[kind][layer, half, rows, cols] = wide(held[at // per, at % per])
                at += 1

    stages = (do_one, do_two, do_scatter, do_spread, do_swap, do_last)
    for t in range(many + len(stages) - 1):
        for n, stage in enumerate(stages):
            if 0 <= t - n < many:
                stage(t - n)
    for group in (stage_a, one, two, stage_e):
        for copy in group.values():
            copy.wait_send()
    for group in (stage_c, stage_d):
        for copies in group.values():
            for copy in copies:
                copy.wait_send()


def reduce_all(grads, shards, replicas):
    layers = len(grads)
    deep = replicas // 2
    ins, plan, groups = [], [], []
    for layer in reversed(range(layers)):
        qkv, out, up, down = grads[layer][:4]
        cut = (qkv.shape[1] + out.shape[1]) // 2
        order = [[(3, down, 0), (2, up, 0)], [(0, qkv[:, :cut], 0), (0, qkv[:, cut:], cut), (1, out, 0)]]
        for part in order:
            group = []
            for kind, g, start in part:
                group.append(len(ins))
                plan.append((kind, layer, start))
                ins.append(
                    g.astype(jnp.bfloat16).reshape(shards, 2, g.shape[0] // shards // 2, g.shape[1])
                )
            if len(group) == 3:
                group = [group[0], group[1], None, group[2]]
            groups.append(group)
    smalls = []
    for layer in range(layers):
        gg, gb, gu = grads[layer][4:]
        width = gg.shape[1] // shards
        smalls.append(jnp.concatenate([
            gg.reshape(-1, shards, width).transpose(1, 0, 2),
            gb.reshape(-1, shards, width).transpose(1, 0, 2),
            gu.reshape(shards, -1, width),
        ], 1))
    ng, nb = grads[0][4].shape[0], grads[0][5].shape[0]
    small = jnp.concatenate(smalls, 1)
    rows = small.shape[1]
    half = rows // 2
    small = small.reshape(shards, 2, half, width).astype(jnp.bfloat16)
    small = jnp.pad(small, ((0, 0), (0, 0), (0, -half % BLOCK), (0, -width % 128)))
    groups[-1].append(len(ins))
    plan.append((4, 0, 0))
    ins.append(small)
    count = len(ins)
    turns = [None] * count
    for group in groups:
        for n, a in enumerate(group):
            if a is not None:
                turns[a] = n % 2
    groups = [[a for a in group if a is not None] for group in groups]
    shapes = [x.shape for x in ins]
    pers = [-(-sum(len(blocks_of(shapes[a][2:])) for a in group) // deep) for group in groups]
    many = len(groups)
    sems = pltpu.SemaphoreType.DMA
    vmem = lambda *s: pltpu.VMEM(s, jnp.bfloat16)
    out_shapes = [
        (layers, 2, g.shape[0] // shards // 2, g.shape[1]) for g in grads[0][:4]
    ] + [(1,) + shapes[-1][1:]]
    outs = pl.pallas_call(
        functools.partial(reduce_kernel, shards, deep, plan, groups, pers, turns),
        out_shape=[jax.ShapeDtypeStruct(s, jnp.float32) for s in out_shapes],
        in_specs=[pl.BlockSpec(memory_space=pltpu.VMEM)] * count,
        out_specs=[pl.BlockSpec(memory_space=pltpu.VMEM)] * len(out_shapes),
        scratch_shapes=[vmem(s[0], *s[2:]) for s in shapes]
        + [vmem(3, *s[2:]) for s in shapes]
        + [vmem(3, *s[2:]) for s in shapes]
        + [vmem(deep, per, BLOCK, 128) for per in pers]
        + [vmem(deep - 1, per, BLOCK, 128) for per in pers]
        + [vmem(per, BLOCK, 128) for per in pers]
        + [vmem(deep, per, BLOCK, 128) for per in pers]
        + [vmem(deep, per, BLOCK, 128) for per in pers]
        + [
            sems((count,)), sems((count,)),
            sems((count, 2)), sems((count, 2)),
            sems((many, deep - 1)), sems((many, deep - 1)),
            sems((many, deep - 1)), sems((many, deep - 1)),
            sems((many,)), sems((many,)), sems((many,)),
        ],
        compiler_params=pltpu.CompilerParams(
            collective_id=1, has_side_effects=True, vmem_limit_bytes=56 * 1024 * 1024
        ),
        name="reduce_grads",
    )(*ins)
    big = [x.reshape(layers, -1, x.shape[3]) for x in outs[:4]]
    tiny = outs[-1][0, :, :half, :width].reshape(layers, rows // layers, width)
    return tuple(big) + (
        tiny[:, :ng],
        tiny[:, ng : ng + nb],
        tiny[:, ng + nb :].reshape(layers, -1),
    )


def on_device(shards, replicas, images, cotangent, counts, *stacks):
    slot_count = images.shape[0]
    live = (jnp.arange(slot_count, dtype=jnp.int32) < counts[0]).astype(jnp.float32)[:, None, None]
    params = gather(stacks, shards)
    kept = []
    stream = images
    for layer in range(LAYERS):
        stream, saved = forward_layer(stream, params[layer])
        kept.append(saved)
    activations = stream * live
    grad = (cotangent * live).reshape(-1, D)
    grads = [None] * LAYERS
    for layer in reversed(range(LAYERS)):
        grad, grads[layer] = backward_layer(kept[layer], grad, params[layer])
    totals = reduce_all(grads, shards, replicas)
    return (activations, grad.reshape(images.shape)) + totals


def solution(mesh):
    in_specs = (
        P(("shard", "replica"), None, None),
        P(("shard", "replica"), None, None),
        P(("shard", "replica")),
        P(None, "shard", None),
        P(None, "shard", None),
        P(None, "shard", None),
        P(None, "shard", None),
        P(None, None, "shard"),
        P(None, None, "shard"),
        P(None, "shard"),
    )
    out_specs = (
        P(("shard", "replica"), None, None),
        P(("shard", "replica"), None, None),
        P(None, "shard", None),
        P(None, "shard", None),
        P(None, "shard", None),
        P(None, "shard", None),
        P(None, None, "shard"),
        P(None, None, "shard"),
        P(None, "shard"),
    )
    return jax.shard_map(
        functools.partial(on_device, mesh.shape["shard"], mesh.shape["replica"]), mesh=mesh, in_specs=in_specs, out_specs=out_specs, check_vma=False
    )
```

```python
import functools

import jax
import jax.numpy as jnp
from jax import lax
from jax.experimental import pallas as pl
from jax.experimental.pallas import tpu as pltpu
from jax.sharding import PartitionSpec as P

D = 384
HEADS = 6
HD = 64
S = 197
LAYERS = 2


EPS = 1e-06
INV_ROOT_TWO = 0.7071067811865476
INV_ROOT_TWO_PI = 0.3989422804014327


def normalize(values, gain, shift):
    center = jnp.mean(values, -1, keepdims=True)
    centered = values - center
    spread = jnp.mean(centered * centered, -1, keepdims=True)
    inverse = lax.rsqrt(spread + EPS)
    unit = centered * inverse
    return (unit * gain + shift, unit, inverse)


def norm_back(upstream, unit, inverse, gain):
    scaled = upstream * gain
    inner = (
        scaled
        - jnp.mean(scaled, -1, keepdims=True)
        - unit * jnp.mean(scaled * unit, -1, keepdims=True)
    )
    return (inverse * inner, jnp.sum(upstream * unit, 0), jnp.sum(upstream, 0))


def normal_cdf(values):
    return 0.5 * (1.0 + jax.scipy.special.erf(values * INV_ROOT_TWO))


def product(left, right):
    return jnp.dot(left, right, preferred_element_type=jnp.float32)


def product_left(left, right):
    return lax.dot_general(
        left, right, (((0,), (0,)), ((), ())), preferred_element_type=jnp.float32
    )


def product_right(left, right):
    return lax.dot_general(
        left, right, (((1,), (1,)), ((), ())), preferred_element_type=jnp.float32
    )


def batched(form, left, right):
    return jnp.einsum(form, left, right, preferred_element_type=jnp.float32)


def forward_layer(stream, params):
    w_qkv, w_out, w_up, w_down, gains, biases, up_bias = params
    gains = gains.astype(jnp.float32)
    biases = biases.astype(jnp.float32)
    up_bias = up_bias.astype(jnp.float32)
    blocks = stream.shape[0]
    factor = HD ** (-0.5)
    rows_in = stream.reshape(-1, D)
    normed_f, unit_one, scale_one = normalize(rows_in, gains[0], biases[0])
    normed_one = normed_f.astype(jnp.bfloat16)
    project = product(normed_one, w_qkv)
    queries = (
        ((project[:, :D] + biases[1]) * factor).astype(jnp.bfloat16).reshape(blocks, S, HEADS, HD)
    )
    key_rows = project[:, D : 2 * D].astype(jnp.bfloat16).reshape(blocks, S, HEADS, HD)
    values = (project[:, 2 * D :] + biases[2]).astype(jnp.bfloat16).reshape(blocks, S, HEADS, HD)
    scores = batched("bqhe,bkhe->bhqk", queries, key_rows)
    log_total = jnp.log(jnp.sum(jnp.exp(scores), -1, keepdims=True))
    probs = jnp.exp(scores - log_total)
    prob_low = probs.astype(jnp.bfloat16)
    mixed = batched("bhqk,bkhe->bqhe", prob_low, values).reshape(-1, D).astype(jnp.bfloat16)
    middle = rows_in + product(mixed, w_out) + biases[3]
    normed_g, unit_two, scale_two = normalize(middle, gains[1], biases[4])
    normed_two = normed_g.astype(jnp.bfloat16)
    hidden = product(normed_two, w_up) + up_bias
    activated = (hidden * normal_cdf(hidden)).astype(jnp.bfloat16)
    result = middle + product(activated, w_down) + biases[5]
    saved = (
        normed_one,
        unit_one,
        scale_one,
        queries,
        key_rows,
        values,
        log_total,
        mixed,
        normed_two,
        unit_two,
        scale_two,
        hidden,
        activated,
    )
    return (result.reshape(stream.shape), saved)


def backward_layer(saved, grad, params):
    w_qkv, w_out, w_up, w_down, gains, biases, up_bias = params
    gains_f = gains.astype(jnp.float32)
    factor = HD ** (-0.5)
    (
        normed_one,
        unit_one,
        scale_one,
        queries,
        key_rows,
        values,
        log_total,
        mixed,
        normed_two,
        unit_two,
        scale_two,
        hidden,
        activated,
    ) = saved
    blocks = queries.shape[0]
    low = grad.astype(jnp.bfloat16)
    down_grad = product_left(activated, low)
    shift_five = jnp.sum(grad, 0)
    act_grad = product_right(low, w_down)
    dens = jnp.exp(-0.5 * hidden * hidden) * INV_ROOT_TWO_PI
    hid_grad = act_grad * (normal_cdf(hidden) + hidden * dens)
    hid_low = hid_grad.astype(jnp.bfloat16)
    up_grad = product_left(normed_two, hid_low)
    upbias_grad = jnp.sum(hid_grad, 0)
    norm_grad = product_right(hid_low, w_up)
    back_two, gain_two, shift_four = norm_back(norm_grad, unit_two, scale_two, gains_f[1])
    mid_grad = grad + back_two
    mid_low = mid_grad.astype(jnp.bfloat16)
    out_grad = product_left(mixed, mid_low)
    shift_three = jnp.sum(mid_grad, 0)
    mixed_grad = product_right(mid_low, w_out).astype(jnp.bfloat16).reshape(blocks, S, HEADS, HD)
    scores = batched("bqhe,bkhe->bhqk", queries, key_rows)
    probs = jnp.exp(scores - log_total)
    prob_low = probs.astype(jnp.bfloat16)
    prob_grad = batched("bqhe,bkhe->bhqk", mixed_grad, values)
    row_dot = jnp.sum(probs * prob_grad, -1, keepdims=True)
    score_grad = (probs * (prob_grad - row_dot)).astype(jnp.bfloat16)
    query_grad = (batched("bhqk,bkhe->bqhe", score_grad, key_rows) * factor).reshape(-1, D)
    key_grad = batched("bhqk,bqhe->bkhe", score_grad, queries).reshape(-1, D)
    value_grad = batched("bhqk,bqhe->bkhe", prob_low, mixed_grad).reshape(-1, D)
    project_grad = jnp.concatenate([query_grad, key_grad, value_grad], 1).astype(jnp.bfloat16)
    qkv_grad = product_left(normed_one, project_grad)
    first_grad = product_right(project_grad, w_qkv)
    back_one, gain_one, shift_zero = norm_back(first_grad, unit_one, scale_one, gains_f[0])
    stream_grad = mid_grad + back_one
    grads = (
        qkv_grad,
        out_grad,
        up_grad,
        down_grad,
        jnp.stack([gain_one, gain_two], 0),
        jnp.stack(
            [
                shift_zero,
                jnp.sum(query_grad, 0),
                jnp.sum(value_grad, 0),
                shift_three,
                shift_four,
                shift_five,
            ],
            0,
        ),
        upbias_grad,
    )
    return (stream_grad, grads)


MESH = pl.DeviceIdType.MESH


def place(shards, replicas):
    me = lax.axis_index("shard")
    rep = lax.axis_index("replica")
    core = lax.rem(rep, 2)
    depth = lax.div(rep, 2)
    return me, rep, core, depth, rep + 1 - 2 * core


def gather_kernel(shards, layers, count, *refs):
    ins, outs = refs[: count + 1], refs[count + 1 : count + 2 + layers * count]
    send, recv, psend, precv, zsend, zrecv, qsend, qrecv, ssend, srecv, local = refs[
        count + 2 + layers * count :
    ]
    me, rep, core, depth, mate = place(shards, 0)
    parity = lax.rem(depth, 2)
    across = (depth + 1 - 2 * parity) * 2 + core
    side = (me + 1 - 2 * lax.rem(me, 2), lax.rem(me + 2, shards))
    far = shards - 1 - me
    barrier = pltpu.get_barrier_semaphore()
    pl.semaphore_signal(barrier, inc=1, device_id=(me, mate), device_id_type=MESH)
    pl.semaphore_signal(barrier, inc=1, device_id=(me, across), device_id_type=MESH)
    for k in range(1, shards):
        peer = lax.rem(me + k, shards)
        pl.semaphore_signal(barrier, inc=1, device_id=(peer, rep), device_id_type=MESH)
    pl.semaphore_wait(barrier, shards + 1)

    def work(odd):
        started = []

        def remote(src, dst, send_sem, recv_sem, device):
            copy = pltpu.make_async_remote_copy(
                src_ref=src, dst_ref=dst, send_sem=send_sem, recv_sem=recv_sem, device_id=device,
                device_id_type=MESH)
            copy.start()
            started.append(copy)
            return copy

        small_in, small_out = ins[count], outs[layers * count]
        swapped = [(a, odd) for a in (2, 0, 1)]
        items = swapped + [(3, layer) for layer in range(layers)]
        first = []
        for item, (a, layer) in enumerate(items):
            for k in range(2):
                first.append(remote(
                    ins[a].at[layer, core], outs[layer * count + a].at[me, core], send.at[item, k],
                    recv.at[item, k], (side[k], rep)))
        smalls = []
        for k in range(1, shards):
            peer = lax.rem(me + k, shards)
            smalls.append(remote(
                small_in, small_out.at[me], ssend.at[k - 1], srecv.at[k - 1], (peer, rep)))
        own = []
        for a in range(count):
            for layer in range(layers):
                copy = pltpu.make_async_copy(
                    ins[a].at[layer], outs[layer * count + a].at[me], local.at[a * layers + layer])
                copy.start()
                own.append(copy)
        copy = pltpu.make_async_copy(small_in, small_out.at[me], local.at[layers * count])
        copy.start()
        own.append(copy)
        passed, crossed = [], []

        def hand_on(item, slot, origin):
            a, layer = items[item]
            piece = outs[layer * count + a].at[origin, core]
            if item < len(swapped):
                copy = remote(piece, piece, zsend.at[item, slot], zrecv.at[item, slot], (me, across))
                crossed.append((item, slot, origin, copy))
            passed.append(
                remote(piece, piece, psend.at[item, slot], precv.at[item, slot], (me, mate)))

        relays = []
        for item in range(len(items) + 1):
            if item < len(items):
                a, layer = items[item]
                via = item % 2
                for k in (via, 1 - via):
                    first[2 * item + k].wait_recv()
                    if k == via:
                        piece = outs[layer * count + a].at[side[via], core]
                        relays.append(remote(
                            piece, piece, send.at[item, 2], recv.at[item, 2], (side[1 - via], rep)))
                    hand_on(item, k, side[k])
            if item > 0:
                relays[item - 1].wait_recv()
                hand_on(item - 1, 2, far)
        for item, slot, origin, copy in crossed:
            copy.wait_recv()
            piece = outs[(1 - odd) * count + items[item][0]].at[origin, core]
            passed.append(
                remote(piece, piece, qsend.at[item, slot], qrecv.at[item, slot], (me, mate)))
        for copy in smalls + passed:
            copy.wait_recv()
        for copy in own:
            copy.wait()
        for copy in started:
            copy.wait_send()

    for odd in range(2):
        pl.when(parity == odd)(functools.partial(work, odd))


def gather(stacks, shards):
    weights = stacks[:4]
    layers = weights[0].shape[0]
    ins = [w.reshape(layers, 2, w.shape[1] // 2, w.shape[2]) for w in weights]
    gains, biases, up_bias = stacks[4:]
    width = gains.shape[2]
    small = jnp.concatenate([gains, biases, up_bias.reshape(layers, -1, width)], 1)
    rows = small.shape[1]
    small = jnp.pad(small, ((0, 0), (0, -rows % 16), (0, -width % 128)))
    count = len(ins)
    shapes = [
        jax.ShapeDtypeStruct((shards,) + w.shape[1:], w.dtype) for _ in range(layers) for w in ins
    ]
    shapes.append(jax.ShapeDtypeStruct((shards,) + small.shape, small.dtype))
    sems = pltpu.SemaphoreType.DMA
    table = sems((count - 1 + layers, shards - 1))
    cross = sems((count - 1, shards - 1))
    outs = pl.pallas_call(
        functools.partial(gather_kernel, shards, layers, count),
        out_shape=shapes,
        in_specs=[pl.BlockSpec(memory_space=pltpu.VMEM)] * (count + 1),
        out_specs=[pl.BlockSpec(memory_space=pl.ANY)] * len(shapes),
        scratch_shapes=[table] * 4 + [cross] * 4
        + [sems((shards - 1,)), sems((shards - 1,)), sems((layers * count + 1,))],
        compiler_params=pltpu.CompilerParams(collective_id=0, has_side_effects=True),
        name="gather_params",
    )(*ins, small)
    tiny = outs[-1][:, :, :rows, :width]
    params = []
    for layer in range(layers):
        big = [outs[layer * count + a].reshape(-1, weights[a].shape[2]) for a in range(count)]
        part = tiny[:, layer]
        ng, nb = gains.shape[1], biases.shape[1]
        params.append(tuple(big) + (
            part[:, :ng].transpose(1, 0, 2).reshape(ng, -1),
            part[:, ng : ng + nb].transpose(1, 0, 2).reshape(nb, -1),
            part[:, ng + nb :].reshape(-1),
        ))
    return params


BLOCK = 48


def blocks_of(shape):
    return [(r, c) for r in range(shape[0] // BLOCK) for c in range(shape[1] // 128)]


def reduce_kernel(shards, deep, plan, groups, pers, turn, *refs):
    count = len(plan)
    kinds = 1 + max(kind for kind, _, _ in plan)
    many = len(groups)
    ins, outs = refs[:count], refs[count : count + kinds]
    refs = refs[count + kinds :]
    buf_a, buf_s, buf_b = refs[:count], refs[count : 2 * count], refs[2 * count : 3 * count]
    z_own, z_recv, z_sum, z_all, z_mate = [
        refs[3 * count + n * many : 3 * count + (n + 1) * many] for n in range(5)
    ]
    a_send, a_recv, b_send, b_recv, c_send, c_recv, d_send, d_recv, e_send, e_recv, loc = refs[
        3 * count + 5 * many :
    ]
    me, rep, core, depth, mate = place(shards, deep)
    side = (me + 1 - 2 * lax.rem(me, 2), lax.rem(me + 2, shards))
    far = shards - 1 - me
    barrier = pltpu.get_barrier_semaphore()
    pl.semaphore_signal(barrier, inc=1, device_id=(me, mate), device_id_type=MESH)
    for k in range(2):
        pl.semaphore_signal(barrier, inc=1, device_id=(side[k], rep), device_id_type=MESH)
    for k in range(1, deep):
        peer = lax.rem(depth + k, deep) * 2 + core
        pl.semaphore_signal(barrier, inc=1, device_id=(me, peer), device_id_type=MESH)
    pl.semaphore_wait(barrier, deep + 2)

    def wide(value):
        return value.astype(jnp.float32)

    def remote(src, dst, send, recv, device):
        copy = pltpu.make_async_remote_copy(
            src_ref=src, dst_ref=dst, send_sem=send, recv_sem=recv, device_id=device,
            device_id_type=MESH)
        copy.start()
        return copy

    stage_a = {}
    for group in groups:
        for a in group:
            stage_a[a] = remote(
                ins[a].at[:, 1 - core], buf_a[a], a_send.at[a], a_recv.at[a], (me, mate))
    one, two, stage_c, stage_d, stage_e = {}, {}, {}, {}, {}

    def pair(a, dest):
        return wide(ins[a][dest, core]) + wide(buf_a[a][dest])

    def do_one(g):
        for a in groups[g]:
            stage_a[a].wait_recv()
            near = side[turn[a]]
            buf_s[a][0] = pair(a, near).astype(jnp.bfloat16)
            buf_s[a][1] = pair(a, far).astype(jnp.bfloat16)
            one[a] = remote(
                buf_s[a].at[pl.ds(0, 2)], buf_b[a].at[pl.ds(0, 2)], b_send.at[a, 0],
                b_recv.at[a, 0], (near, rep))

    def do_two(g):
        for a in groups[g]:
            one[a].wait_recv()
            near = side[1 - turn[a]]
            buf_s[a][2] = (pair(a, near) + wide(buf_b[a][1])).astype(jnp.bfloat16)
            two[a] = remote(
                buf_s[a].at[2], buf_b[a].at[2], b_send.at[a, 1], b_recv.at[a, 1], (near, rep))

    def do_scatter(g):
        per, number = pers[g], 0
        for a in groups[g]:
            two[a].wait_recv()
            for r, c in blocks_of(buf_a[a].shape[1:]):
                rows, cols = pl.ds(r * BLOCK, BLOCK), pl.ds(c * 128, 128)
                total = wide(ins[a][me, core, rows, cols]) + wide(buf_a[a][me, rows, cols])
                total = total + wide(buf_b[a][0, rows, cols]) + wide(buf_b[a][2, rows, cols])
                z_own[g][number // per, number % per] = total.astype(jnp.bfloat16)
                number += 1
        while number < deep * per:
            z_own[g][number // per, number % per] = jnp.zeros((BLOCK, 128), jnp.bfloat16)
            number += 1
        stage_c[g] = []
        for k in range(1, deep):
            peer = lax.rem(depth + k, deep)
            stage_c[g].append(remote(
                z_own[g].at[peer], z_recv[g].at[k - 1], c_send.at[g, k - 1],
                c_recv.at[g, k - 1], (me, peer * 2 + core)))

    def do_spread(g):
        for copy in stage_c[g]:
            copy.wait_recv()
        for b in range(pers[g]):
            total = wide(z_own[g][depth, b])
            for k in range(deep - 1):
                total = total + wide(z_recv[g][k, b])
            z_sum[g][b] = total.astype(jnp.bfloat16)
        stage_d[g] = []
        for k in range(1, deep):
            peer = lax.rem(depth + k, deep)
            stage_d[g].append(remote(
                z_sum[g], z_all[g].at[depth], d_send.at[g, k - 1], d_recv.at[g, k - 1],
                (me, peer * 2 + core)))
        own = pltpu.make_async_copy(z_sum[g], z_all[g].at[depth], loc.at[g])
        own.start()
        own.wait()

    def do_swap(g):
        for copy in stage_d[g]:
            copy.wait_recv()
        stage_e[g] = remote(z_all[g], z_mate[g], e_send.at[g], e_recv.at[g], (me, mate))
        put(g, z_all[g], core)

    def do_last(g):
        stage_e[g].wait_recv()
        put(g, z_mate[g], 1 - core)

    def put(g, held, half):
        per, at = pers[g], 0
        for a in groups[g]:
            kind, layer, start = plan[a]
            for r, c in blocks_of(buf_a[a].shape[1:]):
                rows, cols = pl.ds(r * BLOCK, BLOCK), pl.ds(start + c * 128, 128)
                outs[kind][layer, half, rows, cols] = wide(held[at // per, at % per])
                at += 1

    stages = (do_one, do_two, do_scatter, do_spread, do_swap, do_last)
    for t in range(many + len(stages) - 1):
        for n, stage in enumerate(stages):
            if 0 <= t - n < many:
                stage(t - n)
    for group in (stage_a, one, two, stage_e):
        for copy in group.values():
            copy.wait_send()
    for group in (stage_c, stage_d):
        for copies in group.values():
            for copy in copies:
                copy.wait_send()


def reduce_all(grads, shards, replicas):
    layers = len(grads)
    deep = replicas // 2
    ins, plan, groups = [], [], []
    for layer in reversed(range(layers)):
        qkv, out, up, down = grads[layer][:4]
        cut = (qkv.shape[1] + out.shape[1]) // 2
        order = [[(3, down, 0), (2, up, 0)], [(0, qkv[:, :cut], 0), (0, qkv[:, cut:], cut), (1, out, 0)]]
        for part in order:
            group = []
            for kind, g, start in part:
                group.append(len(ins))
                plan.append((kind, layer, start))
                ins.append(
                    g.astype(jnp.bfloat16).reshape(shards, 2, g.shape[0] // shards // 2, g.shape[1])
                )
            if len(group) == 3:
                group = [group[0], group[1], None, group[2]]
            groups.append(group)
    smalls = []
    for layer in range(layers):
        gg, gb, gu = grads[layer][4:]
        width = gg.shape[1] // shards
        smalls.append(jnp.concatenate([
            gg.reshape(-1, shards, width).transpose(1, 0, 2),
            gb.reshape(-1, shards, width).transpose(1, 0, 2),
            gu.reshape(shards, -1, width),
        ], 1))
    ng, nb = grads[0][4].shape[0], grads[0][5].shape[0]
    small = jnp.concatenate(smalls, 1)
    rows = small.shape[1]
    half = rows // 2
    small = small.reshape(shards, 2, half, width).astype(jnp.bfloat16)
    small = jnp.pad(small, ((0, 0), (0, 0), (0, -half % BLOCK), (0, -width % 128)))
    groups[-1].append(len(ins))
    plan.append((4, 0, 0))
    ins.append(small)
    count = len(ins)
    turns = [None] * count
    for group in groups:
        for n, a in enumerate(group):
            if a is not None:
                turns[a] = n % 2
    groups = [[a for a in group if a is not None] for group in groups]
    shapes = [x.shape for x in ins]
    pers = [-(-sum(len(blocks_of(shapes[a][2:])) for a in group) // deep) for group in groups]
    many = len(groups)
    sems = pltpu.SemaphoreType.DMA
    vmem = lambda *s: pltpu.VMEM(s, jnp.bfloat16)
    out_shapes = [
        (layers, 2, g.shape[0] // shards // 2, g.shape[1]) for g in grads[0][:4]
    ] + [(1,) + shapes[-1][1:]]
    outs = pl.pallas_call(
        functools.partial(reduce_kernel, shards, deep, plan, groups, pers, turns),
        out_shape=[jax.ShapeDtypeStruct(s, jnp.float32) for s in out_shapes],
        in_specs=[pl.BlockSpec(memory_space=pltpu.VMEM)] * count,
        out_specs=[pl.BlockSpec(memory_space=pltpu.VMEM)] * len(out_shapes),
        scratch_shapes=[vmem(s[0], *s[2:]) for s in shapes]
        + [vmem(3, *s[2:]) for s in shapes]
        + [vmem(3, *s[2:]) for s in shapes]
        + [vmem(deep, per, BLOCK, 128) for per in pers]
        + [vmem(deep - 1, per, BLOCK, 128) for per in pers]
        + [vmem(per, BLOCK, 128) for per in pers]
        + [vmem(deep, per, BLOCK, 128) for per in pers]
        + [vmem(deep, per, BLOCK, 128) for per in pers]
        + [
            sems((count,)), sems((count,)),
            sems((count, 2)), sems((count, 2)),
            sems((many, deep - 1)), sems((many, deep - 1)),
            sems((many, deep - 1)), sems((many, deep - 1)),
            sems((many,)), sems((many,)), sems((many,)),
        ],
        compiler_params=pltpu.CompilerParams(
            collective_id=1, has_side_effects=True, vmem_limit_bytes=56 * 1024 * 1024
        ),
        name="reduce_grads",
    )(*ins)
    big = [x.reshape(layers, -1, x.shape[3]) for x in outs[:4]]
    tiny = outs[-1][0, :, :half, :width].reshape(layers, rows // layers, width)
    return tuple(big) + (
        tiny[:, :ng],
        tiny[:, ng : ng + nb],
        tiny[:, ng + nb :].reshape(layers, -1),
    )


def on_device(shards, replicas, images, cotangent, counts, *stacks):
    slot_count = images.shape[0]
    live = (jnp.arange(slot_count, dtype=jnp.int32) < counts[0]).astype(jnp.float32)[:, None, None]
    params = gather(stacks, shards)
    kept = []
    stream = images
    for layer in range(LAYERS):
        stream, saved = forward_layer(stream, params[layer])
        kept.append(saved)
    activations = stream * live
    grad = (cotangent * live).reshape(-1, D)
    grads = [None] * LAYERS
    for layer in reversed(range(LAYERS)):
        grad, grads[layer] = backward_layer(kept[layer], grad, params[layer])
    totals = reduce_all(grads, shards, replicas)
    return (activations, grad.reshape(images.shape)) + totals


def solution(mesh):
    in_specs = (
        P(("shard", "replica"), None, None),
        P(("shard", "replica"), None, None),
        P(("shard", "replica")),
        P(None, "shard", None),
        P(None, "shard", None),
        P(None, "shard", None),
        P(None, "shard", None),
        P(None, None, "shard"),
        P(None, None, "shard"),
        P(None, "shard"),
    )
    out_specs = (
        P(("shard", "replica"), None, None),
        P(("shard", "replica"), None, None),
        P(None, "shard", None),
        P(None, "shard", None),
        P(None, "shard", None),
        P(None, "shard", None),
        P(None, None, "shard"),
        P(None, None, "shard"),
        P(None, "shard"),
    )
    return jax.shard_map(
        functools.partial(on_device, mesh.shape["shard"], mesh.shape["replica"]), mesh=mesh, in_specs=in_specs, out_specs=out_specs, check_vma=False
    )
```
